32 devices in a mesh: seq: 16 (over z, y, core), head: 2 (over x).
Axes of the slice: x: 2, y: 2, z: 4, core: 2. Of those that a mesh axis runs over, the one named last changes fastest.
Arguments:
- tokens: bfloat16 [512, 2048], P('seq', 'head'), may hold values from -6 to 6
- ln1_gain: float32 [2048], replicated, may hold values from 0.1 to 1.9
- ln1_shift: float32 [2048], replicated, may hold values from -1.75 to 1.75
- ln2_gain: float32 [2048], replicated, may hold values from 0.1 to 1.9
- ln2_shift: float32 [2048], replicated, may hold values from -1.75 to 1.75
- w_qkv: bfloat16 [2048, 3, 2048], P(None, None, 'head'), may hold values from -0.125 to 0.125
- b_qkv: float32 [3, 2048], P(None, 'head'), may hold values from -3 to 3
- w_dense: bfloat16 [2048, 2048], P('head'), may hold values from -0.125 to 0.125
- b_dense: float32 [2048], P('head'), may hold values from -1.75 to 1.75
- w_up: bfloat16 [2048, 4096], P(None, 'head'), may hold values from -0.125 to 0.125
- b_up: float32 [4096], P('head'), may hold values from -3 to 3
- w_down: bfloat16 [4096, 2048], P('head'), may hold values from -0.09375 to 0.09375
- b_down: float32 [2048], P('head'), may hold values from -1.75 to 1.75
- keys_short: bfloat16 [512, 64, 2048], P('seq', None, 'head'), may hold values from -210 to 210
- values_short: bfloat16 [512, 64, 2048], P('seq', None, 'head'), may hold values from -16 to 16
- keys_long: bfloat16 [32768, 2048], P('seq', 'head'), may hold values from -210 to 210
- values_long: bfloat16 [32768, 2048], P('seq', 'head'), may hold values from -16 to 16
- lengths: int32 [512], replicated, may hold values from 16 to 8192, as said below
- slot_request: int32 [512], replicated, may hold values from 0 to 511, as said below
- piece_map: int32 [16], replicated, may hold values from 0 to 15, each once
Outputs:
- layer_out: bfloat16 [512, 2048], P('seq', 'head')
The draws below stay inside these ranges and needn't reach their ends.
Inputs may be any that keep to these rules, and one draw needn't show every extreme that they name: `lengths`: requests 0 to 3 hold more than 4096 positions, one of them exactly 8192; every other request holds 16 to 64 positions, one of them exactly 64. `slot_request`: A permutation of the requests; slot s lies on index s // 32 of seq. The requests 32 h to 32 h + 31 are served in 8 groups of exactly 4 on as many different indices of seq. Rows 2048 b to 2048 b + 2047 of keys_long and values_long hold positions (piece_map[b] % 4) * 2048 onwards of the cache of request piece_map[b] // 4.
All inputs are finite; a program needn't handle non-finite values.
Results may differ from the reference program's by a relative error of at most 0.0095.
Values may be sent and summed in bfloat16 or wider, within the bound.
A program may use at most 192 MiB of HBM per device.

```python
import jax
import jax.numpy as jnp
from jax import lax

D = 2048
HEADS = 8
HD = 256
FF = 4096
ROT = 64
SHORT_MAX = 64
LONGS = 4
CAP = 4
RPD = 32
PIECE_LEN = 2048
REQS = 512
PIECES = 4
LONG_MAX = 8192
N_SEQ = 16


def draw_lengths(key, part):
    key_short, key_spot, key_long, key_top = jax.random.split(key, 4)
    indices = jnp.arange(REQS, dtype=jnp.int32)
    short_len = jax.random.randint(key_short, (REQS,), SHORT_MAX // 4, SHORT_MAX + 1, dtype=jnp.int32)
    short_spot = jax.random.randint(key_spot, (), LONGS, REQS, dtype=jnp.int32)
    short_len = jnp.where(indices == short_spot, SHORT_MAX, short_len)
    long_len = jax.random.randint(key_long, (REQS,), LONG_MAX // 2 + 1, LONG_MAX + 1, dtype=jnp.int32)
    long_spot = jax.random.randint(key_top, (), 0, LONGS, dtype=jnp.int32)
    long_len = jnp.where(indices == long_spot, LONG_MAX, long_len)
    return jnp.where(indices < LONGS, long_len, short_len).astype(jnp.int32)


def draw_slot_request(key, part):
    keys_all = jax.random.split(key, 5)
    groups = RPD // CAP
    shuffle_home = jax.random.permutation(keys_all[0], N_SEQ)
    shuffle_owner = jax.random.permutation(keys_all[1], N_SEQ)
    offsets = jax.random.permutation(keys_all[2], N_SEQ)[:groups]
    orders = jax.vmap(lambda sub_key: jax.random.permutation(sub_key, RPD))(jax.random.split(keys_all[3], N_SEQ))
    group_of = orders // CAP
    homes = jnp.arange(N_SEQ, dtype=jnp.int32)[:, None]
    owners = shuffle_owner[(shuffle_home[homes] + offsets[group_of]) % N_SEQ]
    tiebreak = jax.random.permutation(keys_all[4], REQS)
    scores = owners.reshape(REQS).astype(jnp.int32) * REQS + tiebreak.astype(jnp.int32)
    return jnp.argsort(scores).astype(jnp.int32)


def key_field(key, count, length):
    key_base = jax.random.fold_in(key, 0)
    base = jnp.clip(jax.random.normal(key_base, (count, length, D), jnp.float32), -6.0, 6.0) * 2.5
    return base


def draw_keys_short(key, part):
    return key_field(key, REQS, SHORT_MAX).astype(jnp.bfloat16)


def draw_keys_long(key, part):
    return key_field(key, N_SEQ, PIECE_LEN).reshape(N_SEQ * PIECE_LEN, D).astype(jnp.bfloat16)


def level_of(stream_key, shape, cuts, smallest, top_value):
    level, own = 1.0, jax.random.fold_in(stream_key, 6)
    for dim, blocks in cuts:
        draws = jnp.exp(jax.random.uniform(jax.random.fold_in(own, dim), (blocks,), jnp.float32, smallest / len(cuts), top_value / len(cuts)))
        level = level * jnp.repeat(draws, shape[dim] // blocks).reshape([-1 if axis == dim else 1 for axis in range(len(shape))])
    return level


def gaussian(own_key, extent, scale, limit, cuts=(), kind=jnp.bfloat16):
    drawn = scale * jax.random.normal(own_key, extent, jnp.float32)
    if cuts:
        drawn = drawn * level_of(own_key, extent, cuts, -0.22, 0.18)
    return jnp.clip(drawn, -limit, limit).astype(kind)


def setup_inputs(seed: int = 0) -> dict:
    arg_keys = jax.random.split(jax.random.key(seed), 21)
    return {
        "tokens": gaussian(arg_keys[0], (REQS, D), 1.0, 6.0, ((0, 16), (1, 2))),
        "ln1_gain": jnp.clip(1.0 + 0.18 * jax.random.normal(arg_keys[1], (D,), jnp.float32), 0.1, 1.9),
        "ln1_shift": gaussian(arg_keys[2], (D,), 0.3, 1.75, (), jnp.float32),
        "ln2_gain": jnp.clip(1.0 + 0.18 * jax.random.normal(arg_keys[3], (D,), jnp.float32), 0.1, 1.9),
        "ln2_shift": gaussian(arg_keys[4], (D,), 0.3, 1.75, (), jnp.float32),
        "w_qkv": gaussian(arg_keys[5], (D, 3, D), D ** -0.5, 0.125, ((2, 2),)),
        "b_qkv": gaussian(arg_keys[6], (3, D), 0.5, 3.0, ((1, 2),), jnp.float32),
        "w_dense": gaussian(arg_keys[7], (D, D), D ** -0.5, 0.125, ((0, 2),)),
        "b_dense": gaussian(arg_keys[8], (D,), 0.3, 1.75, ((0, 2),), jnp.float32),
        "w_up": gaussian(arg_keys[9], (D, FF), D ** -0.5, 0.125, ((1, 2),)),
        "b_up": gaussian(arg_keys[10], (FF,), 0.5, 3.0, ((0, 2),), jnp.float32),
        "w_down": gaussian(arg_keys[11], (FF, D), FF ** -0.5, 0.09375, ((0, 2),)),
        "b_down": gaussian(arg_keys[12], (D,), 0.3, 1.75, ((0, 2),), jnp.float32),
        "keys_short": draw_keys_short(jax.random.fold_in(arg_keys[20], 71), 0),
        "values_short": gaussian(arg_keys[14], (REQS, SHORT_MAX, D), 3.0, 16.0, ((0, 16), (2, 2))),
        "keys_long": draw_keys_long(jax.random.fold_in(arg_keys[20], 71), 0),
        "values_long": gaussian(arg_keys[16], (PIECE_LEN * N_SEQ, D), 3.0, 16.0, ((0, 16), (1, 2))),
        "lengths": draw_lengths(jax.random.fold_in(arg_keys[20], 71), 0),
        "slot_request": draw_slot_request(jax.random.fold_in(arg_keys[20], 71), 0),
        "piece_map": jax.random.permutation(arg_keys[19], N_SEQ).astype(jnp.int32),
    }


epsilon = 1e-05
very_low = -1e+30

def layer_norm(values, gain, shift):
    center = lax.optimization_barrier(jnp.mean(values, axis=-1, keepdims=True))
    offset = values - center
    spread = lax.optimization_barrier(jnp.mean(offset * offset, axis=-1, keepdims=True))
    return offset * lax.rsqrt(spread + epsilon) * gain + shift

def rotary(values, position):
    half_rot = ROT // 2
    frequency = jnp.power(10000.0, -2.0 * jnp.arange(half_rot, dtype=jnp.float32) / ROT).astype(jnp.float32)
    angles = position.astype(jnp.float32)[:, None] * frequency[None, :]
    cosine = jnp.cos(angles)[:, None, :]
    sine_of = jnp.sin(angles)[:, None, :]
    leading = values[..., :half_rot]
    trailing = values[..., half_rot:ROT]
    return jnp.concatenate([leading * cosine - trailing * sine_of, trailing * cosine + leading * sine_of, values[..., ROT:]], axis=-1)

def attend(queries, key_rows, value_rows, usable):
    scores = jnp.einsum('rhc,rthc->rht', queries.astype(jnp.float32), key_rows.astype(jnp.float32), precision=lax.Precision.HIGHEST) * HD ** (-0.5)
    masked = jnp.where(usable[:, None, :], scores, very_low)
    summit = lax.optimization_barrier(jnp.max(masked, axis=-1))
    weights = jnp.where(usable[:, None, :], jnp.exp(masked - summit[..., None]), 0.0)
    amount = lax.optimization_barrier(jnp.sum(weights, axis=-1))
    rounded = lax.optimization_barrier(weights.astype(jnp.bfloat16))
    mixed = jnp.einsum('rht,rthc->rhc', rounded.astype(jnp.float32), value_rows.astype(jnp.float32), precision=lax.Precision.HIGHEST)
    return (summit, amount, mixed)

def reference(tokens, ln1_gain, ln1_shift, ln2_gain, ln2_shift, w_qkv, b_qkv, w_dense, b_dense, w_up, b_up, w_down, b_down, keys_short, values_short, keys_long, values_long, lengths, slot_request, piece_map):
    total = slot_request.shape[0]
    resident = tokens[slot_request].astype(jnp.float32)
    slot_len = lengths[slot_request]
    normed_attn = layer_norm(resident, ln1_gain, ln1_shift).astype(jnp.bfloat16)
    normed_mlp = layer_norm(resident, ln2_gain, ln2_shift).astype(jnp.bfloat16)
    projected = jnp.dot(normed_attn, w_qkv.reshape(D, 3 * D), preferred_element_type=jnp.float32).reshape(total, 3, D) + b_qkv[None]
    queries = rotary(projected[:, 0].reshape(total, HEADS, HD), slot_len).astype(jnp.bfloat16)
    new_keys = rotary(projected[:, 1].reshape(total, HEADS, HD), slot_len).astype(jnp.bfloat16)
    new_values = projected[:, 2].reshape(total, HEADS, HD).astype(jnp.bfloat16)
    short_usable = (jnp.arange(SHORT_MAX, dtype=jnp.int32)[None, :] < slot_len[:, None]) & (slot_len <= SHORT_MAX)[:, None]
    short_top, short_total, short_out = attend(queries, keys_short.reshape(total, SHORT_MAX, HEADS, HD), values_short.reshape(total, SHORT_MAX, HEADS, HD), short_usable)
    own_score = lax.optimization_barrier(jnp.sum(queries.astype(jnp.float32) * new_keys.astype(jnp.float32), axis=-1)) * HD ** (-0.5)
    inverse = jnp.argsort(slot_request).astype(jnp.int32)
    long_query = queries[inverse[:LONGS]]
    long_owner = (piece_map // PIECES).astype(jnp.int32)
    piece_index = piece_map % PIECES
    piece_query = long_query[long_owner]
    positions = piece_index[:, None] * PIECE_LEN + jnp.arange(PIECE_LEN, dtype=jnp.int32)[None, :]
    piece_usable = positions < lengths[long_owner][:, None]
    piece_top, piece_total, piece_out = attend(piece_query, keys_long.reshape(N_SEQ, PIECE_LEN, HEADS, HD), values_long.reshape(N_SEQ, PIECE_LEN, HEADS, HD), piece_usable)
    matches = slot_request[:, None] == long_owner[None, :]
    spread_top = jnp.where(matches[:, :, None], piece_top[None], very_low)
    summit = jnp.maximum(jnp.maximum(short_top, own_score), lax.optimization_barrier(jnp.max(spread_top, axis=1)))
    piece_scale = jnp.where(matches[:, :, None], jnp.exp(piece_top[None] - summit[:, None]), 0.0)
    short_scale = jnp.exp(short_top - summit)
    own_scale = jnp.exp(own_score - summit)
    denominator = short_total * short_scale + own_scale + lax.optimization_barrier(jnp.sum(piece_scale * piece_total[None], axis=1))
    numerator = short_out * short_scale[..., None] + new_values.astype(jnp.float32) * own_scale[..., None]
    numerator = numerator + jnp.einsum('rdh,dhc->rhc', piece_scale, piece_out, precision=lax.Precision.HIGHEST)
    attended = (numerator / denominator[..., None]).reshape(total, D).astype(jnp.bfloat16)
    hidden_units = jax.nn.gelu(jnp.dot(normed_mlp, w_up, preferred_element_type=jnp.float32) + b_up, approximate=False).astype(jnp.bfloat16)
    finished = resident + jnp.dot(attended, w_dense, preferred_element_type=jnp.float32) + jnp.dot(hidden_units, w_down, preferred_element_type=jnp.float32) + b_dense + b_down
    finished = finished.astype(jnp.bfloat16)
    return jnp.zeros((total, D), jnp.bfloat16).at[slot_request].set(finished)
```

```python
import functools

import jax
import jax.numpy as jnp
from jax import lax
from jax.experimental import pallas as pl
from jax.experimental.pallas import tpu as pltpu
from jax.sharding import PartitionSpec as P

HD = 256
ROT = 64
LONGS = 4
CAP = 4
MESH = pl.DeviceIdType.MESH

epsilon = 1e-05
very_low = -1e30


def layer_norm(values, gain, shift):
    center = jnp.mean(values, axis=-1, keepdims=True)
    offset = values - center
    spread = jnp.mean(offset * offset, axis=-1, keepdims=True)
    return offset * lax.rsqrt(spread + epsilon) * gain + shift


def rotary(values, position):
    half_rot = ROT // 2
    frequency = jnp.power(10000.0, -2.0 * jnp.arange(half_rot, dtype=jnp.float32) / ROT)
    angles = position.astype(jnp.float32)[:, None] * frequency[None, :]
    cosine = jnp.cos(angles)[:, None, :]
    sine_of = jnp.sin(angles)[:, None, :]
    leading = values[..., :half_rot]
    trailing = values[..., half_rot:ROT]
    return jnp.concatenate(
        [
            leading * cosine - trailing * sine_of,
            trailing * cosine + leading * sine_of,
            values[..., ROT:],
        ],
        axis=-1,
    )


def attend(queries, key_rows, value_rows, usable):
    scores = jnp.einsum(
        "rhc,rthc->rht", queries, key_rows, preferred_element_type=jnp.float32
    ) * HD ** (-0.5)
    masked = jnp.where(usable[:, None, :], scores, very_low)
    summit = jnp.max(masked, axis=-1)
    weights = jnp.where(usable[:, None, :], jnp.exp(masked - summit[..., None]), 0.0)
    amount = jnp.sum(weights, axis=-1)
    mixed = jnp.einsum(
        "rht,rthc->rhc",
        weights.astype(jnp.bfloat16),
        value_rows,
        preferred_element_type=jnp.float32,
    )
    return (summit, amount, mixed)


def device_of(flat, seqs):
    return (lax.rem(flat, seqs), lax.div(flat, seqs))


def greet(me, total, seqs):
    barrier = pltpu.get_barrier_semaphore()

    def hello(k, carry):
        other = lax.rem(me + k, total)
        pl.semaphore_signal(
            barrier, inc=1, device_id=device_of(other, seqs), device_id_type=MESH
        )
        return carry

    lax.fori_loop(1, total, hello, 0)
    pl.semaphore_wait(barrier, total - 1)


def dispatch_kernel(seqs, heads, rows_ref, long_ref, recv_ref, lrecv_ref, ssem, rsem, lssem, lrsem):
    total = seqs * heads
    seq = lax.axis_index("seq")
    head = lax.axis_index("head")
    me = head * seqs + seq
    greet(me, total, seqs)

    def rows_copy(target, source):
        return pltpu.make_async_remote_copy(
            src_ref=rows_ref.at[lax.rem(target, seqs)],
            dst_ref=recv_ref.at[source],
            send_sem=ssem.at[target],
            recv_sem=rsem.at[source],
            device_id=device_of(target, seqs),
            device_id_type=MESH,
        )

    def long_copy(target, source_head):
        return pltpu.make_async_remote_copy(
            src_ref=long_ref,
            dst_ref=lrecv_ref.at[source_head],
            send_sem=lssem.at[target],
            recv_sem=lrsem.at[source_head],
            device_id=device_of(target, seqs),
            device_id_type=MESH,
        )

    def send(k, carry):
        rows_copy(lax.rem(me + k, total), me).start()
        return carry

    def send_long(k, carry):
        long_copy(lax.rem(me + k, total), head).start()
        return carry

    @pl.when(seq == 0)
    def _():
        lax.fori_loop(1, total, send_long, 0)

    lax.fori_loop(1, total, send, 0)
    recv_ref[me] = rows_ref[seq]

    @pl.when(seq == 0)
    def _():
        lrecv_ref[head] = long_ref[...]

    def finish(k, carry):
        rows_copy(lax.rem(me + k, total), me).wait_send()
        rows_copy(me, lax.rem(me + total - k, total)).wait_recv()
        return carry

    lax.fori_loop(1, total, finish, 0)

    def sent_long(k, carry):
        long_copy(lax.rem(me + k, total), head).wait_send()
        return carry

    @pl.when(seq == 0)
    def _():
        lax.fori_loop(1, total, sent_long, 0)

    for source_head in range(heads):

        @pl.when(jnp.logical_or(seq != 0, head != source_head))
        def _():
            long_copy(me, source_head).wait_recv()


def pieces_kernel(seqs, heads, part_ref, recv_ref, ssem, rsem):
    seq = lax.axis_index("seq")
    head = lax.axis_index("head")
    barrier = pltpu.get_barrier_semaphore()

    def hello(k, carry):
        pl.semaphore_signal(
            barrier, inc=1, device_id=(lax.rem(seq + k, seqs), head), device_id_type=MESH
        )
        return carry

    lax.fori_loop(1, seqs, hello, 0)
    pl.semaphore_wait(barrier, seqs - 1)

    def copy(target, source):
        return pltpu.make_async_remote_copy(
            src_ref=part_ref,
            dst_ref=recv_ref.at[source],
            send_sem=ssem.at[target],
            recv_sem=rsem.at[source],
            device_id=(target, head),
            device_id_type=MESH,
        )

    def send(k, carry):
        copy(lax.rem(seq + k, seqs), seq).start()
        return carry

    lax.fori_loop(1, seqs, send, 0)
    recv_ref[seq] = part_ref[...]

    def finish(k, carry):
        copy(lax.rem(seq + k, seqs), seq).wait_send()
        copy(seq, lax.rem(seq + seqs - k, seqs)).wait_recv()
        return carry

    lax.fori_loop(1, seqs, finish, 0)


def return_kernel(seqs, heads, rows_ref, recv_ref, ssem, rsem):
    total = seqs * heads
    seq = lax.axis_index("seq")
    head = lax.axis_index("head")
    me = head * seqs + seq
    greet(me, total, seqs)

    def copy(target, source):
        return pltpu.make_async_remote_copy(
            src_ref=rows_ref.at[target],
            dst_ref=recv_ref.at[source],
            send_sem=ssem.at[target],
            recv_sem=rsem.at[source],
            device_id=device_of(target, seqs),
            device_id_type=MESH,
        )

    def send(k, carry):
        copy(lax.rem(me + k, total), me).start()
        return carry

    lax.fori_loop(1, total, send, 0)
    recv_ref[me] = rows_ref[me]

    def finish(k, carry):
        copy(lax.rem(me + k, total), me).wait_send()
        copy(me, lax.rem(me + total - k, total)).wait_recv()
        return carry

    lax.fori_loop(1, total, finish, 0)


def comm_call(kernel, name, out_shapes, sem_counts, collective_id, *operands):
    vmem = pl.BlockSpec(memory_space=pltpu.VMEM)
    return pl.pallas_call(
        kernel,
        out_shape=out_shapes,
        in_specs=[vmem] * len(operands),
        out_specs=jax.tree.map(lambda _: vmem, out_shapes),
        scratch_shapes=[pltpu.SemaphoreType.DMA((count,)) for count in sem_counts],
        compiler_params=pltpu.CompilerParams(
            collective_id=collective_id, has_side_effects=True
        ),
        name=name,
    )(*operands)


def local(
    seqs,
    heads,
    tokens,
    ln1_gain,
    ln1_shift,
    ln2_gain,
    ln2_shift,
    w_qkv,
    b_qkv,
    w_dense,
    b_dense,
    w_up,
    b_up,
    w_down,
    b_down,
    keys_short,
    values_short,
    keys_long,
    values_long,
    lengths,
    slot_request,
    piece_map,
):
    total = seqs * heads
    slot_rows, part_width = tokens.shape
    width = part_width * heads
    seq_place = lax.axis_index("seq")
    heads_here = part_width // HD
    slots = jnp.arange(slot_request.shape[0], dtype=jnp.int32)
    local_ids = jnp.arange(slot_rows, dtype=jnp.int32)
    cells = jnp.arange(seqs * CAP, dtype=jnp.int32)

    home_ids = seq_place * slot_rows + local_ids
    my_owner = (
        jnp.sum(jnp.where(slot_request[None, :] == home_ids[:, None], slots[None, :], 0), axis=1)
        // slot_rows
    )
    home_rank = jnp.sum(
        (my_owner[None, :] == my_owner[:, None]) & (local_ids[None, :] < local_ids[:, None]),
        axis=1,
        dtype=jnp.int32,
    )
    home_cell = my_owner * CAP + home_rank
    home_select = (cells[:, None] == home_cell[None, :]).astype(jnp.bfloat16)
    home_back = (home_cell[:, None] == cells[None, :]).astype(jnp.bfloat16)
    my_requests = lax.dynamic_slice_in_dim(slot_request, seq_place * slot_rows, slot_rows)
    my_home = my_requests // slot_rows
    slot_rank = jnp.sum(
        (my_home[None, :] == my_home[:, None]) & (my_requests[None, :] < my_requests[:, None]),
        axis=1,
        dtype=jnp.int32,
    )
    slot_cell = my_home * CAP + slot_rank
    slot_select = (slot_cell[:, None] == cells[None, :]).astype(jnp.bfloat16)
    slot_back = (cells[:, None] == slot_cell[None, :]).astype(jnp.bfloat16)

    packed = (
        jnp.dot(home_select, tokens, preferred_element_type=jnp.float32)
        .astype(jnp.bfloat16)
        .reshape(seqs, CAP, part_width)
    )
    arrived, long_rows = comm_call(
        functools.partial(dispatch_kernel, seqs, heads),
        "dispatch",
        (
            jax.ShapeDtypeStruct((total, CAP, part_width), jnp.bfloat16),
            jax.ShapeDtypeStruct((heads, LONGS, part_width), jnp.bfloat16),
        ),
        (total, total, total, heads),
        0,
        packed,
        tokens[:LONGS],
    )
    arrived = arrived.reshape(heads, seqs * CAP, part_width)
    resident = jnp.concatenate(
        [
            jnp.concatenate(
                [
                    jnp.dot(slot_select, arrived[h], preferred_element_type=jnp.float32)
                    for h in range(heads)
                ],
                axis=1,
            ),
            jnp.concatenate([long_rows[h] for h in range(heads)], axis=1).astype(jnp.float32),
        ],
        axis=0,
    )
    normed_attn = layer_norm(resident, ln1_gain, ln1_shift).astype(jnp.bfloat16)
    normed_mlp = layer_norm(resident[:slot_rows], ln2_gain, ln2_shift).astype(jnp.bfloat16)
    parts = [
        jnp.dot(normed_attn, w_qkv[:, j], preferred_element_type=jnp.float32) + b_qkv[j][None]
        for j in range(3)
    ]
    my_lengths = jnp.sum(
        jnp.where(my_requests[:, None] == slots[None, :], lengths[None, :], 0), axis=1
    )
    all_lengths = jnp.concatenate([my_lengths, lengths[:LONGS]])
    rows_all = slot_rows + LONGS
    every_query = rotary(parts[0].reshape(rows_all, heads_here, HD), all_lengths).astype(
        jnp.bfloat16
    )
    queries = every_query[:slot_rows]
    long_queries = every_query[slot_rows:]
    new_keys = rotary(
        parts[1][:slot_rows].reshape(slot_rows, heads_here, HD), my_lengths
    ).astype(jnp.bfloat16)
    new_values = parts[2][:slot_rows].reshape(slot_rows, heads_here, HD).astype(jnp.bfloat16)

    piece_count = seqs // LONGS
    my_piece = lax.dynamic_slice_in_dim(piece_map, seq_place, 1)[0]
    long_owner = my_piece // piece_count
    piece_index = my_piece % piece_count
    long_pick = jnp.arange(LONGS, dtype=jnp.int32) == long_owner
    piece_query = jnp.sum(
        jnp.where(long_pick[:, None, None], long_queries.astype(jnp.float32), 0.0), axis=0
    ).astype(jnp.bfloat16)
    long_length = jnp.sum(jnp.where(long_pick, lengths[:LONGS], 0))
    piece_len = keys_long.shape[0]
    positions = piece_index * piece_len + jnp.arange(piece_len, dtype=jnp.int32)
    piece_usable = (positions < long_length)[None, :]
    piece_top, piece_total, piece_out = attend(
        piece_query[None],
        keys_long.reshape(1, piece_len, heads_here, HD),
        values_long.reshape(1, piece_len, heads_here, HD),
        piece_usable,
    )
    stats = jnp.concatenate(
        [
            jnp.broadcast_to(piece_top[0][:, None], (heads_here, 128)),
            jnp.broadcast_to(piece_total[0][:, None], (heads_here, 128)),
        ],
        axis=1,
    )
    every_piece = comm_call(
        functools.partial(pieces_kernel, seqs, heads),
        "pieces",
        jax.ShapeDtypeStruct((seqs, 2 * heads_here, HD), jnp.float32),
        (seqs, seqs),
        1,
        jnp.concatenate([piece_out[0], stats], axis=0),
    )

    short_max = keys_short.shape[1]
    short_usable = (jnp.arange(short_max, dtype=jnp.int32)[None, :] < my_lengths[:, None]) & (
        my_lengths <= short_max
    )[:, None]
    short_top, short_total, short_out = attend(
        queries,
        keys_short.reshape(slot_rows, short_max, heads_here, HD),
        values_short.reshape(slot_rows, short_max, heads_here, HD),
        short_usable,
    )
    own_score = jnp.sum(
        queries.astype(jnp.float32) * new_keys.astype(jnp.float32), axis=-1
    ) * HD ** (-0.5)

    out_of = every_piece[:, :heads_here]
    top_of = every_piece[:, heads_here:, 0]
    total_of = every_piece[:, heads_here:, 128]
    matches = my_requests[:, None] == (piece_map // piece_count)[None, :]
    spread = jnp.where(matches[:, :, None], top_of[None], very_low)
    summit = jnp.maximum(jnp.maximum(short_top, own_score), jnp.max(spread, axis=1))
    piece_scale = jnp.where(matches[:, :, None], jnp.exp(spread - summit[:, None]), 0.0)
    short_scale = jnp.exp(short_top - summit)
    own_scale = jnp.exp(own_score - summit)
    denominator = (
        short_total * short_scale + own_scale + jnp.sum(piece_scale * total_of[None], axis=1)
    )
    numerator = (
        short_out * short_scale[..., None]
        + new_values.astype(jnp.float32) * own_scale[..., None]
        + jnp.sum(piece_scale[..., None] * out_of[None], axis=1)
    )
    attended = (
        (numerator / denominator[..., None]).reshape(slot_rows, part_width).astype(jnp.bfloat16)
    )
    hidden_units = jax.nn.gelu(
        jnp.dot(normed_mlp, w_up, preferred_element_type=jnp.float32) + b_up, approximate=False
    ).astype(jnp.bfloat16)
    partial_sum = (
        jnp.dot(attended, w_dense, preferred_element_type=jnp.float32)
        + jnp.dot(hidden_units, w_down, preferred_element_type=jnp.float32)
    ).astype(jnp.bfloat16)
    outgoing = jnp.stack(
        [
            jnp.dot(
                slot_back,
                partial_sum[:, h * part_width : (h + 1) * part_width],
                preferred_element_type=jnp.float32,
            ).astype(jnp.bfloat16)
            for h in range(heads)
        ]
    ).reshape(total, CAP, part_width)
    returned = comm_call(
        functools.partial(return_kernel, seqs, heads),
        "give_back",
        jax.ShapeDtypeStruct((total, CAP, part_width), jnp.bfloat16),
        (total, total),
        2,
        outgoing,
    ).reshape(heads, seqs * CAP, part_width)
    head_total = sum(
        jnp.dot(home_back, returned[h], preferred_element_type=jnp.float32) for h in range(heads)
    )
    return (tokens.astype(jnp.float32) + head_total + b_dense + b_down).astype(jnp.bfloat16)


def solution(mesh):
    in_specs = (
        P("seq", "head"),
        P(),
        P(),
        P(),
        P(),
        P(None, None, "head"),
        P(None, "head"),
        P("head", None),
        P("head"),
        P(None, "head"),
        P("head"),
        P("head", None),
        P("head"),
        P("seq", None, "head"),
        P("seq", None, "head"),
        P("seq", "head"),
        P("seq", "head"),
        P(),
        P(),
        P(),
    )
    out_specs = P("seq", "head")
    body = functools.partial(local, mesh.shape["seq"], mesh.shape["head"])
    return jax.shard_map(body, mesh=mesh, in_specs=in_specs, out_specs=out_specs, check_vma=False)
```

```python
import functools

import jax
import jax.numpy as jnp
import numpy as np
from jax import lax
from jax.experimental import pallas as pl
from jax.experimental.pallas import tpu as pltpu
from jax.sharding import PartitionSpec as P

HD = 256
ROT = 64
LONGS = 4
CAP = 4
BLOCK = 2 * CAP
PAD = 8
STATS = 128
MESH = pl.DeviceIdType.MESH
F32 = jnp.float32
BF16 = jnp.bfloat16

epsilon = 1e-05
very_low = -1e30


def iota(shape, axis):
    return lax.broadcasted_iota(jnp.int32, shape, axis)


def onehot(mask):
    return jnp.where(mask, 1.0, 0.0).astype(BF16)


def turned(mask):
    return jnp.where(mask, 1.0, 0.0).astype(F32).T.astype(BF16)


def dot(a, b, **kw):
    return jnp.dot(a, b, preferred_element_type=F32, **kw)


def dot_t(a, b):
    return lax.dot_general(a, b, (((1,), (1,)), ((), ())), preferred_element_type=F32)


def at_block(ref, index):
    return ref.at[pl.ds(pl.multiple_of(index * BLOCK, BLOCK), BLOCK)]


def total_of(values, axis):
    return jnp.sum(values, axis=axis, keepdims=True)


def layer_norm(values, gain, shift):
    center = jnp.mean(values, axis=-1, keepdims=True)
    offset = values - center
    spread = jnp.mean(offset * offset, axis=-1, keepdims=True)
    return offset * lax.rsqrt(spread + epsilon) * gain + shift


def matmul_into(out_ref, x_ref, w_ref, tile):
    def step(i, carry):
        cols = pl.ds(pl.multiple_of(i * tile, tile), tile)
        out_ref[:, cols] = dot(x_ref[...], w_ref[:, cols])
        return carry

    lax.fori_loop(0, w_ref.shape[1] // tile, step, 0)


def layer_kernel(
    seqs,
    heads,
    tokens_ref,
    ln1_gain,
    ln1_shift,
    ln2_gain,
    ln2_shift,
    b_qkv,
    b_out,
    b_up,
    lengths_ref,
    slots_row_ref,
    slots_ref,
    pieces_ref,
    freq_ref,
    w_qkv_hbm,
    w_dense_hbm,
    w_up_hbm,
    w_down_hbm,
    ks_hbm,
    vs_hbm,
    kl_hbm,
    vl_hbm,
    out_ref,
    w_qkv,
    w_dense,
    w_up,
    w_down,
    ks,
    vs,
    kl,
    vl,
    pack,
    recv,
    long_pack,
    long_recv,
    part,
    part_recv,
    back,
    back_recv,
    x1,
    x2,
    qkv,
    up,
    hidden,
    attended,
    dense,
    down,
    load_sem,
    self_sem,
    ssem,
    rsem,
    lssem,
    lrsem,
    pssem,
    prsem,
    bssem,
    brsem,
):
    total = seqs * heads
    seq = lax.axis_index("seq")
    head = lax.axis_index("head")
    me = head * seqs + seq
    rows, width_here = tokens_ref.shape
    half = width_here // 2
    heads_here = width_here // HD
    cells = seqs * BLOCK
    requests = slots_row_ref.shape[1]
    short_max = ks.shape[0] // rows
    piece_len = kl.shape[0]
    piece_count = seqs // LONGS

    def device_of(flat):
        return (lax.rem(flat, seqs), lax.div(flat, seqs))

    loads = [
        pltpu.make_async_copy(src, dst, load_sem.at[i])
        for i, (src, dst) in enumerate(
            [
                (w_qkv_hbm.at[0], w_qkv.at[0]),
                (kl_hbm, kl),
                (w_qkv_hbm.at[1], w_qkv.at[1]),
                (w_qkv_hbm.at[2], w_qkv.at[2]),
                (vl_hbm, vl),
                (w_up_hbm, w_up),
                (w_down_hbm, w_down),
                (ks_hbm, ks),
                (vs_hbm, vs),
                (w_dense_hbm, w_dense),
            ]
        )
    ]
    load_q, load_kl, load_k, load_v, load_vl, load_up, load_down, load_ks, load_vs, load_d = loads

    barrier = pltpu.get_barrier_semaphore()

    def hello(k, carry):
        pl.semaphore_signal(
            barrier, inc=1, device_id=device_of(lax.rem(me + k, total)), device_id_type=MESH
        )
        return carry

    lax.fori_loop(1, total, hello, 0)
    for load in loads:
        load.start()

    slots_row = slots_row_ref[...]
    row_ids = iota((rows, 1), 0)
    lanes_all = iota((rows, requests), 1)
    home_ids = row_ids + seq * rows
    position = total_of(jnp.where(slots_row == home_ids, lanes_all, 0), 1)
    my_req = total_of(jnp.where(lanes_all == home_ids, slots_row, 0), 1)
    my_len = total_of(jnp.where(lanes_all == my_req, lengths_ref[...], 0), 1)
    req_row = slots_ref[pl.ds(seq, 1), :]
    group = iota((rows, seqs), 1)
    in_owner = (position >= group * rows) & (position < (group + 1) * rows)
    in_home = (my_req >= group * rows) & (my_req < (group + 1) * rows)
    owner_hot = onehot(in_owner)
    home_hot = onehot(in_home)
    col_ids = iota((rows, rows), 1)
    rank_home = total_of(
        jnp.where(col_ids < row_ids, dot_t(owner_hot, owner_hot), 0.0), 1
    ).astype(jnp.int32)
    rank_slot = total_of(
        jnp.where(req_row < my_req, dot_t(home_hot, home_hot), 0.0), 1
    ).astype(jnp.int32)
    home_cell = total_of(jnp.where(in_owner, group, 0), 1) * BLOCK + rank_home
    slot_cell = total_of(jnp.where(in_home, group, 0), 1) * BLOCK + rank_slot
    lanes = iota((rows, cells), 1)
    home_lo, home_hi = lanes == home_cell, lanes == home_cell + CAP
    slot_lo, slot_hi = lanes == slot_cell, lanes == slot_cell + CAP

    tok = tokens_ref[...]
    pack[...] = (dot(turned(home_lo), tok[:, :half]) + dot(turned(home_hi), tok[:, half:])).astype(
        BF16
    )
    place = iota((BLOCK, rows), 0)
    source_row = iota((BLOCK, rows), 1)
    long_pack[...] = (
        dot(onehot((source_row == place) & (place < LONGS)), tok[:, :half])
        + dot(onehot((source_row + LONGS == place) & (place >= LONGS)), tok[:, half:])
    ).astype(BF16)

    pl.semaphore_wait(barrier, total - 1)

    def rows_copy(target, source):
        return pltpu.make_async_remote_copy(
            src_ref=at_block(pack, lax.rem(target, seqs)),
            dst_ref=at_block(recv, source),
            send_sem=ssem.at[target],
            recv_sem=rsem.at[source],
            device_id=device_of(target),
            device_id_type=MESH,
        )

    def long_copy(target, source_head):
        return pltpu.make_async_remote_copy(
            src_ref=long_pack,
            dst_ref=at_block(long_recv, source_head),
            send_sem=lssem.at[target],
            recv_sem=lrsem.at[source_head],
            device_id=device_of(target),
            device_id_type=MESH,
        )

    def send_long(k, carry):
        long_copy(lax.rem(me + k, total), head).start()
        return carry

    @pl.when(seq == 0)
    def _():
        lax.fori_loop(1, total, send_long, 0)
        own_long = pltpu.make_async_copy(long_pack, at_block(long_recv, head), self_sem.at[0])
        own_long.start()
        own_long.wait()

    def send(k, carry):
        rows_copy(lax.rem(me + k, total), me).start()
        return carry

    lax.fori_loop(1, total, send, 0)
    own_rows = pltpu.make_async_copy(at_block(pack, seq), at_block(recv, me), self_sem.at[1])
    own_rows.start()

    request_lanes = iota((1, requests), 1)
    my_piece = total_of(jnp.where(iota((1, seqs), 1) == seq, pieces_ref[...], 0), 1)
    long_owner = jnp.zeros_like(my_piece)
    for k in range(1, LONGS):
        long_owner = long_owner + jnp.where(my_piece >= k * piece_count, 1, 0)
    piece_index = my_piece - long_owner * piece_count
    long_len = total_of(jnp.where(request_lanes == long_owner, lengths_ref[...], 0), 1)
    long_limit = long_len - piece_index * piece_len

    all_len = jnp.concatenate([my_len, jnp.broadcast_to(long_len, (PAD, 1))], axis=0)
    angles = all_len.astype(F32) * freq_ref[...]
    lane128 = iota(angles.shape, 1)
    cosine = jnp.where(lane128 < ROT, jnp.cos(angles), 1.0)
    sine = jnp.sin(angles)
    sine_a = jnp.where(lane128 < ROT // 2, -sine, 0.0)
    sine_b = jnp.where((lane128 >= ROT // 2) & (lane128 < ROT), sine, 0.0)

    def spread_table(table, rest):
        filler = jnp.full((table.shape[0], HD - 128), rest, F32)
        return jnp.concatenate([table, filler] * heads_here, axis=1)

    cosine = spread_table(cosine, 1.0)
    sine_a = spread_table(sine_a, 0.0)
    sine_b = spread_table(sine_b, 0.0)

    def rotary(values, n):
        return (
            values * cosine[:n]
            + pltpu.roll(values, width_here - ROT // 2, 1) * sine_a[:n]
            + pltpu.roll(values, ROT // 2, 1) * sine_b[:n]
        )

    own_rows.wait()

    def arrive(k, carry):
        rows_copy(me, lax.rem(me + total - k, total)).wait_recv()
        return carry

    lax.fori_loop(1, total, arrive, 0)
    for source_head in range(heads):

        @pl.when(jnp.logical_or(seq != 0, head != source_head))
        def _():
            long_copy(me, source_head).wait_recv()

    pick_lo, pick_hi = onehot(slot_lo), onehot(slot_hi)
    row8, col8 = iota((PAD, BLOCK), 0), iota((PAD, BLOCK), 1)
    long_lo = onehot((row8 == 0) & (col8 == long_owner))
    long_hi = onehot((row8 == 0) & (col8 == long_owner + LONGS))
    columns = []
    long_columns = []
    for h in range(heads):
        block = recv[h * cells : (h + 1) * cells, :]
        lblock = long_recv[h * BLOCK : (h + 1) * BLOCK, :]
        columns += [dot(pick_lo, block), dot(pick_hi, block)]
        long_columns += [dot(long_lo, lblock), dot(long_hi, lblock)]
    resident = jnp.concatenate(
        [jnp.concatenate(columns, axis=1), jnp.concatenate(long_columns, axis=1)], axis=0
    )
    x1[...] = layer_norm(resident, ln1_gain[...], ln1_shift[...]).astype(BF16)
    x2[...] = layer_norm(resident[:rows], ln2_gain[...], ln2_shift[...]).astype(BF16)

    scale = HD ** (-0.5)
    load_q.wait()
    matmul_into(qkv.at[0], x1, w_qkv.at[0], TILE)
    query = rotary(qkv[0] + b_qkv[0:1, :], rows + PAD)
    lane_here = iota((PAD, width_here), 1)
    head_row = iota((PAD, width_here), 0)
    own_lanes = (lane_here >= head_row * HD) & (lane_here < (head_row + 1) * HD)
    long_query = jnp.where(own_lanes, query[rows : rows + 1], 0.0).astype(BF16)
    query = query[:rows].astype(BF16)
    load_kl.wait()
    scores = dot_t(long_query, kl[...]) * scale
    usable = iota(scores.shape, 1) < long_limit
    masked = jnp.where(usable, scores, very_low)
    piece_top = jnp.max(masked, axis=1, keepdims=True)
    weights = jnp.where(usable, jnp.exp(masked - piece_top), 0.0)
    piece_total = total_of(weights, 1)
    load_vl.wait()
    mixed = dot(weights.astype(BF16), vl[...])
    rowh = iota((PAD, HD), 0)
    piece_out = jnp.zeros((PAD, HD), F32)
    for h in range(heads_here):
        piece_out = jnp.where(rowh == h, mixed[:, h * HD : (h + 1) * HD], piece_out)
    stat_lane = iota((PAD, STATS), 1)
    part[...] = jnp.concatenate(
        [piece_out, jnp.where(stat_lane < STATS // 2, piece_top, piece_total)], axis=1
    )

    def part_copy(target, source):
        return pltpu.make_async_remote_copy(
            src_ref=part,
            dst_ref=at_block(part_recv, source),
            send_sem=pssem.at[target],
            recv_sem=prsem.at[source],
            device_id=(target, head),
            device_id_type=MESH,
        )

    def send_part(k, carry):
        part_copy(lax.rem(seq + k, seqs), seq).start()
        return carry

    lax.fori_loop(1, seqs, send_part, 0)
    own_part = pltpu.make_async_copy(part, at_block(part_recv, seq), self_sem.at[2])
    own_part.start()

    load_k.wait()
    matmul_into(qkv.at[1], x1, w_qkv.at[1], TILE)
    load_v.wait()
    matmul_into(qkv.at[2], x1, w_qkv.at[2], TILE)
    new_key = rotary(qkv[1][:rows] + b_qkv[1:2, :], rows).astype(BF16)
    new_value = (qkv[2][:rows] + b_qkv[2:3, :]).astype(BF16).astype(F32)
    product = query.astype(F32) * new_key.astype(F32)

    load_up.wait()
    matmul_into(up, x2, w_up, TILE)
    before = up[...] + b_up[...]
    hidden[...] = (0.5 * before * (1.0 + lax.erf(before * (0.5**0.5)))).astype(BF16)
    load_down.wait()
    matmul_into(down, hidden, w_down, TILE)

    lane_q = iota((rows, width_here), 1)
    query32 = query.astype(F32)
    split = jnp.concatenate(
        [
            jnp.where((lane_q >= h * HD) & (lane_q < (h + 1) * HD), query32, 0.0)
            for h in range(heads_here)
        ],
        axis=0,
    ).astype(BF16)
    load_ks.wait()
    scores = dot_t(split, ks[...]) * scale
    first = jnp.concatenate([row_ids * short_max] * heads_here, axis=0)
    count = jnp.where(my_len <= short_max, my_len, 0)
    last = first + jnp.concatenate([count] * heads_here, axis=0)
    column = iota(scores.shape, 1)
    usable = (column >= first) & (column < last)
    masked = jnp.where(usable, scores, very_low)
    short_top = jnp.max(masked, axis=1, keepdims=True)
    weights = jnp.where(usable, jnp.exp(masked - short_top), 0.0)
    short_total = total_of(weights, 1)
    load_vs.wait()
    short_out = dot(weights.astype(BF16), vs[...])

    own_part.wait()

    def part_arrive(k, carry):
        part_copy(seq, lax.rem(seq + seqs - k, seqs)).wait_recv()
        return carry

    lax.fori_loop(1, seqs, part_arrive, 0)
    expand = onehot(
        (iota((seqs, cells), 1) >= BLOCK * iota((seqs, cells), 0))
        & (iota((seqs, cells), 1) < BLOCK * iota((seqs, cells), 0) + BLOCK)
    )
    piece_lane = dot(
        jnp.broadcast_to(pieces_ref[...].astype(F32), (PAD, seqs)).astype(BF16), expand
    )[0:1, :]
    first_lane = my_req.astype(F32) * piece_count
    matches = (piece_lane >= first_lane) & (piece_lane < first_lane + piece_count)
    stats = part_recv[:, HD:].T
    tops, totals = stats[0:1, :], stats[STATS // 2 : STATS // 2 + 1, :]
    place_in = lax.bitwise_and(lanes, BLOCK - 1)
    for h in range(heads_here):
        here = slice(h * HD, (h + 1) * HD)
        band = slice(h * rows, (h + 1) * rows)
        own_score = total_of(product[:, here], 1) * scale
        pick = matches & (place_in == h)
        spread = jnp.where(pick, tops, very_low)
        summit = jnp.maximum(
            jnp.maximum(short_top[band], own_score), jnp.max(spread, axis=1, keepdims=True)
        )
        piece_scale = jnp.where(pick, jnp.exp(spread - summit), 0.0)
        short_scale = jnp.exp(short_top[band] - summit)
        own_scale = jnp.exp(own_score - summit)
        denominator = (
            short_total[band] * short_scale + own_scale + total_of(piece_scale * totals, 1)
        )
        numerator = (
            short_out[band, here] * short_scale
            + new_value[:, here] * own_scale
            + dot(piece_scale, part_recv[:, :HD], precision=lax.Precision.HIGHEST)
        )
        attended[:, here] = (numerator / denominator).astype(BF16)
    load_d.wait()
    matmul_into(dense, attended, w_dense, TILE)

    give_lo, give_hi = turned(slot_lo), turned(slot_hi)
    for h in range(heads):
        cols = slice(h * width_here, h * width_here + half)
        rest = slice(h * width_here + half, (h + 1) * width_here)
        back[h * cells : (h + 1) * cells, :] = (
            dot(give_lo, (dense[:, cols] + down[:, cols]).astype(BF16))
            + dot(give_hi, (dense[:, rest] + down[:, rest]).astype(BF16))
        ).astype(BF16)

    def back_copy(target, source):
        return pltpu.make_async_remote_copy(
            src_ref=at_block(back, target),
            dst_ref=at_block(back_recv, source),
            send_sem=bssem.at[target],
            recv_sem=brsem.at[source],
            device_id=device_of(target),
            device_id_type=MESH,
        )

    def send_back(k, carry):
        back_copy(lax.rem(me + k, total), me).start()
        return carry

    lax.fori_loop(1, total, send_back, 0)
    own_back = pltpu.make_async_copy(at_block(back, me), at_block(back_recv, me), self_sem.at[3])
    own_back.start()

    def sent(k, carry):
        target = lax.rem(me + k, total)
        rows_copy(target, me).wait_send()
        return carry

    lax.fori_loop(1, total, sent, 0)

    def sent_part(k, carry):
        part_copy(lax.rem(seq + k, seqs), seq).wait_send()
        return carry

    lax.fori_loop(1, seqs, sent_part, 0)

    def sent_long(k, carry):
        long_copy(lax.rem(me + k, total), head).wait_send()
        return carry

    @pl.when(seq == 0)
    def _():
        lax.fori_loop(1, total, sent_long, 0)

    own_back.wait()

    def back_arrive(k, carry):
        back_copy(lax.rem(me + k, total), me).wait_send()
        back_copy(me, lax.rem(me + total - k, total)).wait_recv()
        return carry

    lax.fori_loop(1, total, back_arrive, 0)
    take_lo, take_hi = onehot(home_lo), onehot(home_hi)
    low = jnp.zeros((rows, half), F32)
    high = jnp.zeros((rows, half), F32)
    for h in range(heads):
        block = back_recv[h * cells : (h + 1) * cells, :]
        low = low + dot(take_lo, block)
        high = high + dot(take_hi, block)
    finished = tokens_ref[...].astype(F32) + jnp.concatenate([low, high], axis=1)
    out_ref[...] = (finished + b_out[0:1, :] + b_out[1:2, :]).astype(BF16)


TILE = 512


def local(
    seqs,
    heads,
    tokens,
    ln1_gain,
    ln1_shift,
    ln2_gain,
    ln2_shift,
    w_qkv,
    b_qkv,
    w_dense,
    b_dense,
    w_up,
    b_up,
    w_down,
    b_down,
    keys_short,
    values_short,
    keys_long,
    values_long,
    lengths,
    slot_request,
    piece_map,
):
    total = seqs * heads
    rows, width_here = tokens.shape
    width = width_here * heads
    units = w_up.shape[1]
    half = width_here // 2
    short_rows = rows * keys_short.shape[1]
    exponent = -2.0 * (np.arange(128) % (ROT // 2)) / ROT
    freq = jnp.asarray(np.power(10000.0, exponent).astype(np.float32)[None])
    vmem = pl.BlockSpec(memory_space=pltpu.VMEM)
    hbm = pl.BlockSpec(memory_space=pl.ANY)
    dma = pltpu.SemaphoreType.DMA
    return pl.pallas_call(
        functools.partial(layer_kernel, seqs, heads),
        out_shape=jax.ShapeDtypeStruct((rows, width_here), BF16),
        in_specs=[vmem] * 13 + [hbm] * 8,
        out_specs=vmem,
        scratch_shapes=[
            pltpu.VMEM((3, width, width_here), BF16),
            pltpu.VMEM((width_here, width), BF16),
            pltpu.VMEM((width, units), BF16),
            pltpu.VMEM((units, width), BF16),
            pltpu.VMEM((short_rows, width_here), BF16),
            pltpu.VMEM((short_rows, width_here), BF16),
            pltpu.VMEM(keys_long.shape, BF16),
            pltpu.VMEM(values_long.shape, BF16),
            pltpu.VMEM((seqs * BLOCK, half), BF16),
            pltpu.VMEM((total * BLOCK, half), BF16),
            pltpu.VMEM((BLOCK, half), BF16),
            pltpu.VMEM((heads * BLOCK, half), BF16),
            pltpu.VMEM((PAD, HD + STATS), F32),
            pltpu.VMEM((seqs * PAD, HD + STATS), F32),
            pltpu.VMEM((total * BLOCK, half), BF16),
            pltpu.VMEM((total * BLOCK, half), BF16),
            pltpu.VMEM((rows + PAD, width), BF16),
            pltpu.VMEM((rows, width), BF16),
            pltpu.VMEM((3, rows + PAD, width_here), F32),
            pltpu.VMEM((rows, units), F32),
            pltpu.VMEM((rows, units), BF16),
            pltpu.VMEM((rows, width_here), BF16),
            pltpu.VMEM((rows, width), F32),
            pltpu.VMEM((rows, width), F32),
            dma((10,)),
            dma((4,)),
            dma((total,)),
            dma((total,)),
            dma((total,)),
            dma((heads,)),
            dma((seqs,)),
            dma((seqs,)),
            dma((total,)),
            dma((total,)),
        ],
        compiler_params=pltpu.CompilerParams(
            collective_id=0, has_side_effects=True, vmem_limit_bytes=66_500_000
        ),
        name="layer",
    )(
        tokens,
        ln1_gain[None],
        ln1_shift[None],
        ln2_gain[None],
        ln2_shift[None],
        b_qkv,
        jnp.stack([b_dense, b_down]),
        b_up[None],
        lengths[None],
        slot_request[None],
        slot_request.reshape(seqs, rows),
        piece_map[None],
        freq,
        jnp.transpose(w_qkv, (1, 0, 2)),
        w_dense,
        w_up,
        w_down,
        keys_short.reshape(short_rows, width_here),
        values_short.reshape(short_rows, width_here),
        keys_long,
        values_long,
    )


def solution(mesh):
    in_specs = (
        P("seq", "head"),
        P(),
        P(),
        P(),
        P(),
        P(None, None, "head"),
        P(None, "head"),
        P("head", None),
        P("head"),
        P(None, "head"),
        P("head"),
        P("head", None),
        P("head"),
        P("seq", None, "head"),
        P("seq", None, "head"),
        P("seq", "head"),
        P("seq", "head"),
        P(),
        P(),
        P(),
    )
    out_specs = P("seq", "head")
    body = functools.partial(local, mesh.shape["seq"], mesh.shape["head"])
    return jax.shard_map(body, mesh=mesh, in_specs=in_specs, out_specs=out_specs, check_vma=False)
```

```python
import functools

import jax
import jax.numpy as jnp
import numpy as np
from jax import lax
from jax.experimental import pallas as pl
from jax.experimental.pallas import tpu as pltpu
from jax.sharding import PartitionSpec as P

HD = 256
ROT = 64
LONGS = 4
CAP = 4
BLOCK = 2 * CAP
PAD = 8
STATS = 128
MESH = pl.DeviceIdType.MESH
F32 = jnp.float32
BF16 = jnp.bfloat16

epsilon = 1e-05
very_low = -1e30


def iota(shape, axis):
    return lax.broadcasted_iota(jnp.int32, shape, axis)


def onehot(mask):
    return jnp.where(mask, 1.0, 0.0).astype(BF16)


def turned(mask):
    return jnp.where(mask, 1.0, 0.0).astype(F32).T.astype(BF16)


def dot(a, b, **kw):
    return jnp.dot(a, b, preferred_element_type=F32, **kw)


def dot_t(a, b):
    return lax.dot_general(a, b, (((1,), (1,)), ((), ())), preferred_element_type=F32)


def at_block(ref, index):
    return ref.at[pl.ds(pl.multiple_of(index * BLOCK, BLOCK), BLOCK)]


def total_of(values, axis):
    return jnp.sum(values, axis=axis, keepdims=True)


def layer_norm(values, gain, shift):
    center = jnp.mean(values, axis=-1, keepdims=True)
    offset = values - center
    spread = jnp.mean(offset * offset, axis=-1, keepdims=True)
    return offset * lax.rsqrt(spread + epsilon) * gain + shift


def matmul_into(out_ref, x_ref, w_ref, tile):
    def step(i, carry):
        cols = pl.ds(pl.multiple_of(i * tile, tile), tile)
        out_ref[:, cols] = dot(x_ref[...], w_ref[:, cols])
        return carry

    lax.fori_loop(0, w_ref.shape[1] // tile, step, 0)


def layer_kernel(
    seqs,
    heads,
    tokens_hbm,
    slots_hbm,
    lengths_hbm,
    pieces_hbm,
    freq_hbm,
    ln1_gain_hbm,
    ln1_shift_hbm,
    ln2_gain_hbm,
    ln2_shift_hbm,
    b_qkv_hbm,
    b_dense_hbm,
    b_down_hbm,
    b_up_hbm,
    w_qkv_hbm,
    w_dense_hbm,
    w_up_hbm,
    w_down_hbm,
    ks_hbm,
    vs_hbm,
    kl_hbm,
    vl_hbm,
    out_ref,
    tokens_ref,
    slots_row_ref,
    lengths_ref,
    pieces_ref,
    freq_ref,
    ln1_gain,
    ln1_shift,
    ln2_gain,
    ln2_shift,
    b_qkv,
    b_dense,
    b_down,
    b_up,
    w_qkv,
    w_dense,
    w_up,
    w_down,
    ks,
    vs,
    kl,
    vl,
    pack,
    recv,
    long_pack,
    long_recv,
    part,
    part_recv,
    back,
    back_recv,
    x1,
    x2,
    qkv,
    up,
    hidden,
    attended,
    dense,
    down,
    full,
    sums,
    sums_recv,
    small_sem,
    load_sem,
    self_sem,
    gssem,
    grsem,
    mssem,
    mrsem,
    ssem,
    rsem,
    lssem,
    lrsem,
    pssem,
    prsem,
    bssem,
    brsem,
):
    total = seqs * heads
    seq = lax.axis_index("seq")
    head = lax.axis_index("head")
    me = head * seqs + seq
    rows, width_here = tokens_hbm.shape
    half = width_here // 2
    heads_here = width_here // HD
    cells = seqs * BLOCK
    requests = slots_row_ref.shape[1]
    short_max = ks.shape[0] // rows
    piece_len = kl.shape[0]
    piece_count = seqs // LONGS

    def device_of(flat):
        return (lax.rem(flat, seqs), lax.div(flat, seqs))

    loads = [
        pltpu.make_async_copy(src, dst, load_sem.at[i])
        for i, (src, dst) in enumerate(
            [
                (w_up_hbm, w_up),
                (w_down_hbm, w_down),
                (w_qkv_hbm.at[0], w_qkv.at[0]),
                (kl_hbm, kl),
                (vl_hbm, vl),
                (w_qkv_hbm.at[1], w_qkv.at[1]),
                (w_qkv_hbm.at[2], w_qkv.at[2]),
                (ks_hbm, ks),
                (vs_hbm, vs),
                (w_dense_hbm, w_dense),
            ]
        )
    ]
    load_up, load_down, load_q, load_kl, load_vl, load_k, load_v, load_ks, load_vs, load_d = loads
    smalls = [
        pltpu.make_async_copy(src, dst, small_sem.at[i])
        for i, (src, dst) in enumerate(
            [
                (tokens_hbm, tokens_ref),
                (slots_hbm, slots_row_ref),
                (lengths_hbm, lengths_ref),
                (pieces_hbm, pieces_ref),
                (freq_hbm, freq_ref),
                (ln1_gain_hbm, ln1_gain),
                (ln1_shift_hbm, ln1_shift),
                (ln2_gain_hbm, ln2_gain),
                (ln2_shift_hbm, ln2_shift),
                (b_qkv_hbm, b_qkv),
                (b_dense_hbm, b_dense),
                (b_down_hbm, b_down),
                (b_up_hbm, b_up),
            ]
        )
    ]

    barrier = pltpu.get_barrier_semaphore()

    def hello(k, carry):
        pl.semaphore_signal(
            barrier, inc=1, device_id=device_of(lax.rem(me + k, total)), device_id_type=MESH
        )
        return carry

    lax.fori_loop(1, total, hello, 0)
    for load in smalls + loads:
        load.start()
    for load in smalls:
        load.wait()

    slots_row = slots_row_ref[...]
    row_ids = iota((rows, 1), 0)
    lanes_all = iota((rows, requests), 1)
    home_ids = row_ids + seq * rows
    position = total_of(jnp.where(slots_row == home_ids, lanes_all, 0), 1)
    my_req = total_of(jnp.where(lanes_all == home_ids, slots_row, 0), 1)
    my_len = total_of(jnp.where(lanes_all == my_req, lengths_ref[...], 0), 1)
    req_row = total_of(jnp.where(row_ids == iota((rows, rows), 1), my_req, 0), 0)
    group = iota((rows, seqs), 1)
    in_owner = (position >= group * rows) & (position < (group + 1) * rows)
    in_home = (my_req >= group * rows) & (my_req < (group + 1) * rows)
    owner_hot = onehot(in_owner)
    home_hot = onehot(in_home)
    col_ids = iota((rows, rows), 1)
    rank_home = total_of(
        jnp.where(col_ids < row_ids, dot_t(owner_hot, owner_hot), 0.0), 1
    ).astype(jnp.int32)
    rank_slot = total_of(
        jnp.where(req_row < my_req, dot_t(home_hot, home_hot), 0.0), 1
    ).astype(jnp.int32)
    home_cell = total_of(jnp.where(in_owner, group, 0), 1) * BLOCK + rank_home
    slot_cell = total_of(jnp.where(in_home, group, 0), 1) * BLOCK + rank_slot
    lanes = iota((rows, cells), 1)
    home_lo, home_hi = lanes == home_cell, lanes == home_cell + CAP
    slot_lo, slot_hi = lanes == slot_cell, lanes == slot_cell + CAP

    tok = tokens_ref[...]
    pack[...] = (dot(turned(home_lo), tok[:, :half]) + dot(turned(home_hi), tok[:, half:])).astype(
        BF16
    )
    place = iota((BLOCK, rows), 0)
    source_row = iota((BLOCK, rows), 1)
    long_pack[...] = (
        dot(onehot((source_row == place) & (place < LONGS)), tok[:, :half])
        + dot(onehot((source_row + LONGS == place) & (place >= LONGS)), tok[:, half:])
    ).astype(BF16)

    pl.semaphore_wait(barrier, total - 1)

    def at_band(ref, index):
        return ref.at[pl.ds(pl.multiple_of(index * rows, rows), rows)]

    def band_copy(src, dst, source, target, send_sems, recv_sems):
        return pltpu.make_async_remote_copy(
            src_ref=src,
            dst_ref=at_band(dst, source),
            send_sem=send_sems.at[target],
            recv_sem=recv_sems.at[source],
            device_id=(seq, target),
            device_id_type=MESH,
        )

    def full_copy(target, source):
        return band_copy(tokens_ref, full, source, target, gssem, grsem)

    def sums_copy(target, source):
        return band_copy(at_band(sums, target), sums_recv, source, target, mssem, mrsem)

    peers = [lax.rem(head + k, heads) for k in range(1, heads)]
    sources = [lax.rem(head + heads - k, heads) for k in range(1, heads)]
    for peer in peers:
        full_copy(peer, head).start()
    own_full = pltpu.make_async_copy(tokens_ref, at_band(full, head), self_sem.at[4])
    own_full.start()

    def rows_copy(target, source):
        return pltpu.make_async_remote_copy(
            src_ref=at_block(pack, lax.rem(target, seqs)),
            dst_ref=at_block(recv, source),
            send_sem=ssem.at[target],
            recv_sem=rsem.at[source],
            device_id=device_of(target),
            device_id_type=MESH,
        )

    def long_copy(target, source_head):
        return pltpu.make_async_remote_copy(
            src_ref=long_pack,
            dst_ref=at_block(long_recv, source_head),
            send_sem=lssem.at[target],
            recv_sem=lrsem.at[source_head],
            device_id=device_of(target),
            device_id_type=MESH,
        )

    def send_long(k, carry):
        long_copy(lax.rem(me + k, total), head).start()
        return carry

    @pl.when(seq == 0)
    def _():
        lax.fori_loop(1, total, send_long, 0)
        own_long = pltpu.make_async_copy(long_pack, at_block(long_recv, head), self_sem.at[0])
        own_long.start()
        own_long.wait()

    def send(k, carry):
        rows_copy(lax.rem(me + k, total), me).start()
        return carry

    lax.fori_loop(1, total, send, 0)
    own_rows = pltpu.make_async_copy(at_block(pack, seq), at_block(recv, me), self_sem.at[1])
    own_rows.start()

    request_lanes = iota((1, requests), 1)
    my_piece = total_of(jnp.where(iota((1, seqs), 1) == seq, pieces_ref[...], 0), 1)
    long_owner = jnp.zeros_like(my_piece)
    for k in range(1, LONGS):
        long_owner = long_owner + jnp.where(my_piece >= k * piece_count, 1, 0)
    piece_index = my_piece - long_owner * piece_count
    long_len = total_of(jnp.where(request_lanes == long_owner, lengths_ref[...], 0), 1)
    long_limit = long_len - piece_index * piece_len

    all_len = jnp.concatenate([my_len, jnp.broadcast_to(long_len, (PAD, 1))], axis=0)
    angles = all_len.astype(F32) * freq_ref[...]
    lane128 = iota(angles.shape, 1)
    cosine = jnp.where(lane128 < ROT, jnp.cos(angles), 1.0)
    sine = jnp.sin(angles)
    sine_a = jnp.where(lane128 < ROT // 2, -sine, 0.0)
    sine_b = jnp.where((lane128 >= ROT // 2) & (lane128 < ROT), sine, 0.0)

    def spread_table(table, rest):
        filler = jnp.full((table.shape[0], HD - 128), rest, F32)
        return jnp.concatenate([table, filler] * heads_here, axis=1)

    cosine = spread_table(cosine, 1.0)
    sine_a = spread_table(sine_a, 0.0)
    sine_b = spread_table(sine_b, 0.0)

    def rotary(values, n):
        return (
            values * cosine[:n]
            + pltpu.roll(values, width_here - ROT // 2, 1) * sine_a[:n]
            + pltpu.roll(values, ROT // 2, 1) * sine_b[:n]
        )

    own_full.wait()
    for source in sources:
        full_copy(head, source).wait_recv()
    at_home = jnp.concatenate([full[h * rows : (h + 1) * rows, :] for h in range(heads)], axis=1)
    x2[...] = layer_norm(at_home.astype(F32), ln2_gain[...], ln2_shift[...]).astype(BF16)
    load_up.wait()
    matmul_into(up, x2, w_up, TILE)
    before = up[...] + b_up[...]
    hidden[...] = (0.5 * before * (1.0 + lax.erf(before * (0.5**0.5)))).astype(BF16)
    load_down.wait()
    matmul_into(down, hidden, w_down, TILE)
    for h in range(heads):
        sums[h * rows : (h + 1) * rows, :] = down[
            :, h * width_here : (h + 1) * width_here
        ].astype(BF16)

    own_rows.wait()

    def arrive(k, carry):
        rows_copy(me, lax.rem(me + total - k, total)).wait_recv()
        return carry

    lax.fori_loop(1, total, arrive, 0)
    for source_head in range(heads):

        @pl.when(jnp.logical_or(seq != 0, head != source_head))
        def _():
            long_copy(me, source_head).wait_recv()

    pick_lo, pick_hi = onehot(slot_lo), onehot(slot_hi)
    row8, col8 = iota((PAD, BLOCK), 0), iota((PAD, BLOCK), 1)
    long_lo = onehot((row8 == 0) & (col8 == long_owner))
    long_hi = onehot((row8 == 0) & (col8 == long_owner + LONGS))
    columns = []
    long_columns = []
    for h in range(heads):
        block = recv[h * cells : (h + 1) * cells, :]
        lblock = long_recv[h * BLOCK : (h + 1) * BLOCK, :]
        columns += [dot(pick_lo, block), dot(pick_hi, block)]
        long_columns += [dot(long_lo, lblock), dot(long_hi, lblock)]
    resident = jnp.concatenate(
        [jnp.concatenate(columns, axis=1), jnp.concatenate(long_columns, axis=1)], axis=0
    )
    x1[...] = layer_norm(resident, ln1_gain[...], ln1_shift[...]).astype(BF16)

    for peer in peers:
        sums_copy(peer, head).start()
    own_sums = pltpu.make_async_copy(at_band(sums, head), at_band(sums_recv, head), self_sem.at[5])
    own_sums.start()

    scale = HD ** (-0.5)
    load_q.wait()
    matmul_into(qkv.at[0], x1, w_qkv.at[0], TILE)
    query = rotary(qkv[0] + b_qkv[0:1, :], rows + PAD)
    lane_here = iota((PAD, width_here), 1)
    head_row = iota((PAD, width_here), 0)
    own_lanes = (lane_here >= head_row * HD) & (lane_here < (head_row + 1) * HD)
    long_query = jnp.where(own_lanes, query[rows : rows + 1], 0.0).astype(BF16)
    query = query[:rows].astype(BF16)
    load_kl.wait()
    scores = dot_t(long_query, kl[...]) * scale
    usable = iota(scores.shape, 1) < long_limit
    masked = jnp.where(usable, scores, very_low)
    piece_top = jnp.max(masked, axis=1, keepdims=True)
    weights = jnp.where(usable, jnp.exp(masked - piece_top), 0.0)
    piece_total = total_of(weights, 1)
    load_vl.wait()
    mixed = dot(weights.astype(BF16), vl[...])
    rowh = iota((PAD, HD), 0)
    piece_out = jnp.zeros((PAD, HD), F32)
    for h in range(heads_here):
        piece_out = jnp.where(rowh == h, mixed[:, h * HD : (h + 1) * HD], piece_out)
    stat_lane = iota((PAD, STATS), 1)
    part[...] = jnp.concatenate(
        [piece_out, jnp.where(stat_lane < STATS // 2, piece_top, piece_total)], axis=1
    )

    def part_copy(target, source):
        return pltpu.make_async_remote_copy(
            src_ref=part,
            dst_ref=at_block(part_recv, source),
            send_sem=pssem.at[target],
            recv_sem=prsem.at[source],
            device_id=(target, head),
            device_id_type=MESH,
        )

    def send_part(k, carry):
        part_copy(lax.rem(seq + k, seqs), seq).start()
        return carry

    lax.fori_loop(1, seqs, send_part, 0)
    own_part = pltpu.make_async_copy(part, at_block(part_recv, seq), self_sem.at[2])
    own_part.start()

    load_k.wait()
    matmul_into(qkv.at[1], x1, w_qkv.at[1], TILE)
    load_v.wait()
    matmul_into(qkv.at[2], x1, w_qkv.at[2], TILE)
    new_key = rotary(qkv[1][:rows] + b_qkv[1:2, :], rows).astype(BF16)
    new_value = (qkv[2][:rows] + b_qkv[2:3, :]).astype(BF16).astype(F32)
    product = query.astype(F32) * new_key.astype(F32)

    lane_q = iota((rows, width_here), 1)
    query32 = query.astype(F32)
    split = jnp.concatenate(
        [
            jnp.where((lane_q >= h * HD) & (lane_q < (h + 1) * HD), query32, 0.0)
            for h in range(heads_here)
        ],
        axis=0,
    ).astype(BF16)
    load_ks.wait()
    scores = dot_t(split, ks[...]) * scale
    first = jnp.concatenate([row_ids * short_max] * heads_here, axis=0)
    count = jnp.where(my_len <= short_max, my_len, 0)
    last = first + jnp.concatenate([count] * heads_here, axis=0)
    column = iota(scores.shape, 1)
    usable = (column >= first) & (column < last)
    masked = jnp.where(usable, scores, very_low)
    short_top = jnp.max(masked, axis=1, keepdims=True)
    weights = jnp.where(usable, jnp.exp(masked - short_top), 0.0)
    short_total = total_of(weights, 1)
    load_vs.wait()
    short_out = dot(weights.astype(BF16), vs[...])

    own_part.wait()

    def part_arrive(k, carry):
        part_copy(seq, lax.rem(seq + seqs - k, seqs)).wait_recv()
        return carry

    lax.fori_loop(1, seqs, part_arrive, 0)
    expand = onehot(
        (iota((seqs, cells), 1) >= BLOCK * iota((seqs, cells), 0))
        & (iota((seqs, cells), 1) < BLOCK * iota((seqs, cells), 0) + BLOCK)
    )
    piece_lane = dot(
        jnp.broadcast_to(pieces_ref[...].astype(F32), (PAD, seqs)).astype(BF16), expand
    )[0:1, :]
    first_lane = my_req.astype(F32) * piece_count
    matches = (piece_lane >= first_lane) & (piece_lane < first_lane + piece_count)
    stats = part_recv[:, HD:].T
    tops, totals = stats[0:1, :], stats[STATS // 2 : STATS // 2 + 1, :]
    place_in = lax.bitwise_and(lanes, BLOCK - 1)
    for h in range(heads_here):
        here = slice(h * HD, (h + 1) * HD)
        band = slice(h * rows, (h + 1) * rows)
        own_score = total_of(product[:, here], 1) * scale
        pick = matches & (place_in == h)
        spread = jnp.where(pick, tops, very_low)
        summit = jnp.maximum(
            jnp.maximum(short_top[band], own_score), jnp.max(spread, axis=1, keepdims=True)
        )
        piece_scale = jnp.where(pick, jnp.exp(spread - summit), 0.0)
        short_scale = jnp.exp(short_top[band] - summit)
        own_scale = jnp.exp(own_score - summit)
        denominator = (
            short_total[band] * short_scale + own_scale + total_of(piece_scale * totals, 1)
        )
        numerator = (
            short_out[band, here] * short_scale
            + new_value[:, here] * own_scale
            + dot(piece_scale, part_recv[:, :HD], precision=lax.Precision.HIGHEST)
        )
        attended[:, here] = (numerator / denominator).astype(BF16)
    load_d.wait()
    matmul_into(dense, attended, w_dense, TILE)

    give_lo, give_hi = turned(slot_lo), turned(slot_hi)
    for h in range(heads):
        cols = slice(h * width_here, h * width_here + half)
        rest = slice(h * width_here + half, (h + 1) * width_here)
        back[h * cells : (h + 1) * cells, :] = (
            dot(give_lo, dense[:, cols].astype(BF16))
            + dot(give_hi, dense[:, rest].astype(BF16))
        ).astype(BF16)

    def back_copy(target, source):
        return pltpu.make_async_remote_copy(
            src_ref=at_block(back, target),
            dst_ref=at_block(back_recv, source),
            send_sem=bssem.at[target],
            recv_sem=brsem.at[source],
            device_id=device_of(target),
            device_id_type=MESH,
        )

    def send_back(k, carry):
        back_copy(lax.rem(me + k, total), me).start()
        return carry

    lax.fori_loop(1, total, send_back, 0)
    own_back = pltpu.make_async_copy(at_block(back, me), at_block(back_recv, me), self_sem.at[3])
    own_back.start()

    def sent(k, carry):
        target = lax.rem(me + k, total)
        rows_copy(target, me).wait_send()
        return carry

    lax.fori_loop(1, total, sent, 0)

    def sent_part(k, carry):
        part_copy(lax.rem(seq + k, seqs), seq).wait_send()
        return carry

    lax.fori_loop(1, seqs, sent_part, 0)

    def sent_long(k, carry):
        long_copy(lax.rem(me + k, total), head).wait_send()
        return carry

    @pl.when(seq == 0)
    def _():
        lax.fori_loop(1, total, sent_long, 0)

    own_back.wait()
    own_sums.wait()
    for peer in peers:
        full_copy(peer, head).wait_send()
        sums_copy(peer, head).wait_send()
    settled = tokens_ref[...].astype(F32) + b_dense[...] + b_down[...]
    for source in sources:
        sums_copy(head, source).wait_recv()
    for h in range(heads):
        settled = settled + sums_recv[h * rows : (h + 1) * rows, :].astype(F32)

    def back_arrive(k, carry):
        back_copy(lax.rem(me + k, total), me).wait_send()
        back_copy(me, lax.rem(me + total - k, total)).wait_recv()
        return carry

    lax.fori_loop(1, total, back_arrive, 0)
    take_lo, take_hi = onehot(home_lo), onehot(home_hi)
    low = jnp.zeros((rows, half), F32)
    high = jnp.zeros((rows, half), F32)
    for h in range(heads):
        block = back_recv[h * cells : (h + 1) * cells, :]
        low = low + dot(take_lo, block)
        high = high + dot(take_hi, block)
    out_ref[...] = (settled + jnp.concatenate([low, high], axis=1)).astype(BF16)


TILE = 512


def local(
    seqs,
    heads,
    tokens,
    ln1_gain,
    ln1_shift,
    ln2_gain,
    ln2_shift,
    w_qkv,
    b_qkv,
    w_dense,
    b_dense,
    w_up,
    b_up,
    w_down,
    b_down,
    keys_short,
    values_short,
    keys_long,
    values_long,
    lengths,
    slot_request,
    piece_map,
):
    total = seqs * heads
    rows, width_here = tokens.shape
    width = width_here * heads
    units = w_up.shape[1]
    half = width_here // 2
    short_rows = rows * keys_short.shape[1]
    exponent = -2.0 * (np.arange(128) % (ROT // 2)) / ROT
    freq = jnp.asarray(np.power(10000.0, exponent).astype(np.float32)[None])
    vmem = pl.BlockSpec(memory_space=pltpu.VMEM)
    hbm = pl.BlockSpec(memory_space=pl.ANY)
    dma = pltpu.SemaphoreType.DMA
    return pl.pallas_call(
        functools.partial(layer_kernel, seqs, heads),
        out_shape=jax.ShapeDtypeStruct((rows, width_here), BF16),
        in_specs=[hbm] * 21,
        out_specs=vmem,
        scratch_shapes=[
            pltpu.VMEM((rows, width_here), BF16),
            pltpu.VMEM((1, seqs * rows), jnp.int32),
            pltpu.VMEM((1, seqs * rows), jnp.int32),
            pltpu.VMEM((1, seqs), jnp.int32),
            pltpu.VMEM((1, 128), F32),
            pltpu.VMEM((1, width), F32),
            pltpu.VMEM((1, width), F32),
            pltpu.VMEM((1, width), F32),
            pltpu.VMEM((1, width), F32),
            pltpu.VMEM((3, width_here), F32),
            pltpu.VMEM((1, width_here), F32),
            pltpu.VMEM((1, width_here), F32),
            pltpu.VMEM((1, units), F32),
            pltpu.VMEM((3, width, width_here), BF16),
            pltpu.VMEM((width_here, width), BF16),
            pltpu.VMEM((width, units), BF16),
            pltpu.VMEM((units, width), BF16),
            pltpu.VMEM((short_rows, width_here), BF16),
            pltpu.VMEM((short_rows, width_here), BF16),
            pltpu.VMEM(keys_long.shape, BF16),
            pltpu.VMEM(values_long.shape, BF16),
            pltpu.VMEM((seqs * BLOCK, half), BF16),
            pltpu.VMEM((total * BLOCK, half), BF16),
            pltpu.VMEM((BLOCK, half), BF16),
            pltpu.VMEM((heads * BLOCK, half), BF16),
            pltpu.VMEM((PAD, HD + STATS), F32),
            pltpu.VMEM((seqs * PAD, HD + STATS), F32),
            pltpu.VMEM((total * BLOCK, half), BF16),
            pltpu.VMEM((total * BLOCK, half), BF16),
            pltpu.VMEM((rows + PAD, width), BF16),
            pltpu.VMEM((rows, width), BF16),
            pltpu.VMEM((3, rows + PAD, width_here), F32),
            pltpu.VMEM((rows, units), F32),
            pltpu.VMEM((rows, units), BF16),
            pltpu.VMEM((rows, width_here), BF16),
            pltpu.VMEM((rows, width), F32),
            pltpu.VMEM((rows, width), F32),
            pltpu.VMEM((heads * rows, width_here), BF16),
            pltpu.VMEM((heads * rows, width_here), BF16),
            pltpu.VMEM((heads * rows, width_here), BF16),
            dma((13,)),
            dma((10,)),
            dma((6,)),
            dma((heads,)),
            dma((heads,)),
            dma((heads,)),
            dma((heads,)),
            dma((total,)),
            dma((total,)),
            dma((total,)),
            dma((heads,)),
            dma((seqs,)),
            dma((seqs,)),
            dma((total,)),
            dma((total,)),
        ],
        compiler_params=pltpu.CompilerParams(
            collective_id=0, has_side_effects=True, vmem_limit_bytes=66_500_000
        ),
        name="layer",
    )(
        tokens,
        slot_request[None],
        lengths[None],
        piece_map[None],
        freq,
        ln1_gain[None],
        ln1_shift[None],
        ln2_gain[None],
        ln2_shift[None],
        b_qkv,
        b_dense[None],
        b_down[None],
        b_up[None],
        jnp.transpose(w_qkv, (1, 0, 2)),
        w_dense,
        w_up,
        w_down,
        keys_short.reshape(short_rows, width_here),
        values_short.reshape(short_rows, width_here),
        keys_long,
        values_long,
    )


def solution(mesh):
    in_specs = (
        P("seq", "head"),
        P(),
        P(),
        P(),
        P(),
        P(None, None, "head"),
        P(None, "head"),
        P("head", None),
        P("head"),
        P(None, "head"),
        P("head"),
        P("head", None),
        P("head"),
        P("seq", None, "head"),
        P("seq", None, "head"),
        P("seq", "head"),
        P("seq", "head"),
        P(),
        P(),
        P(),
    )
    out_specs = P("seq", "head")
    body = functools.partial(local, mesh.shape["seq"], mesh.shape["head"])
    return jax.shard_map(body, mesh=mesh, in_specs=in_specs, out_specs=out_specs, check_vma=False)
```

```python
import functools

import jax
import jax.numpy as jnp
import numpy as np
from jax import lax
from jax.experimental import pallas as pl
from jax.experimental.pallas import tpu as pltpu
from jax.sharding import PartitionSpec as P

HD = 256
ROT = 64
LONGS = 4
CAP = 4
BLOCK = 2 * CAP
PAD = 8
STATS = 128
MESH = pl.DeviceIdType.MESH
F32 = jnp.float32
BF16 = jnp.bfloat16

epsilon = 1e-05
very_low = -1e30


def iota(shape, axis):
    return lax.broadcasted_iota(jnp.int32, shape, axis)


def onehot(mask):
    return jnp.where(mask, 1.0, 0.0).astype(BF16)


def turned(mask):
    return jnp.where(mask, 1.0, 0.0).astype(F32).T.astype(BF16)


def dot(a, b, **kw):
    return jnp.dot(a, b, preferred_element_type=F32, **kw)


def dot_t(a, b):
    return lax.dot_general(a, b, (((1,), (1,)), ((), ())), preferred_element_type=F32)


def at_block(ref, index):
    return ref.at[pl.ds(pl.multiple_of(index * BLOCK, BLOCK), BLOCK)]


def total_of(values, axis):
    return jnp.sum(values, axis=axis, keepdims=True)


def layer_norm(values, gain, shift):
    center = jnp.mean(values, axis=-1, keepdims=True)
    offset = values - center
    spread = jnp.mean(offset * offset, axis=-1, keepdims=True)
    return offset * lax.rsqrt(spread + epsilon) * gain + shift


def matmul_into(out_ref, x_ref, w_ref, tile):
    tile = min(tile, w_ref.shape[1])

    def step(i, carry):
        cols = pl.ds(pl.multiple_of(i * tile, tile), tile)
        out_ref[:, cols] = dot(x_ref[...], w_ref[:, cols])
        return carry

    lax.fori_loop(0, w_ref.shape[1] // tile, step, 0)


def layer_kernel(
    seqs,
    heads,
    tokens_ref,
    slots_row_ref,
    lengths_ref,
    pieces_ref,
    freq_ref,
    ln1_gain,
    ln1_shift,
    ln2_gain,
    ln2_shift,
    b_qkv,
    b_dense,
    b_down,
    b_up,
    w_qkv_hbm,
    w_dense_hbm,
    w_up_hbm,
    w_down_hbm,
    ks_hbm,
    vs_hbm,
    kl_hbm,
    vl_hbm,
    out_ref,
    w_qkv,
    w_dense,
    w_up,
    w_down,
    ks,
    vs,
    kl,
    vl,
    pack,
    recv,
    long_pack,
    long_recv,
    part,
    part_recv,
    back,
    back_recv,
    x1,
    x2,
    qkv,
    up,
    hidden,
    attended,
    dense,
    down,
    full,
    sums,
    sums_recv,
    load_sem,
    self_sem,
    gssem,
    grsem,
    mssem,
    mrsem,
    ssem,
    rsem,
    lssem,
    lrsem,
    pssem,
    prsem,
    bssem,
    brsem,
):
    total = seqs * heads
    seq = lax.axis_index("seq")
    head = lax.axis_index("head")
    me = head * seqs + seq
    rows, width_here = tokens_ref.shape
    half = width_here // 2
    heads_here = width_here // HD
    cells = seqs * BLOCK
    requests = slots_row_ref.shape[1]
    short_max = ks.shape[0] // rows
    piece_len = kl.shape[0]
    piece_count = seqs // LONGS

    def device_of(flat):
        return (lax.rem(flat, seqs), lax.div(flat, seqs))

    loads = [
        pltpu.make_async_copy(src, dst, load_sem.at[i])
        for i, (src, dst) in enumerate(
            [
                (w_up_hbm, w_up),
                (w_down_hbm, w_down),
                (w_qkv_hbm.at[0], w_qkv.at[0]),
                (kl_hbm, kl),
                (vl_hbm, vl),
                (w_qkv_hbm.at[1], w_qkv.at[1]),
                (w_qkv_hbm.at[2], w_qkv.at[2]),
                (ks_hbm, ks),
                (vs_hbm, vs),
                (w_dense_hbm, w_dense),
            ]
        )
    ]
    load_up, load_down, load_q, load_kl, load_vl, load_k, load_v, load_ks, load_vs, load_d = loads
    barrier = pltpu.get_barrier_semaphore()

    def hello(k, carry):
        pl.semaphore_signal(
            barrier, inc=1, device_id=device_of(lax.rem(me + k, total)), device_id_type=MESH
        )
        return carry

    lax.fori_loop(1, total, hello, 0)
    for load in loads:
        load.start()

    slots_row = slots_row_ref[...]
    row_ids = iota((rows, 1), 0)
    lanes_all = iota((rows, requests), 1)
    home_ids = row_ids + seq * rows
    position = total_of(jnp.where(slots_row == home_ids, lanes_all, 0), 1)
    my_req = total_of(jnp.where(lanes_all == home_ids, slots_row, 0), 1)
    my_len = total_of(jnp.where(lanes_all == my_req, lengths_ref[...], 0), 1)
    req_row = total_of(jnp.where(row_ids == iota((rows, rows), 1), my_req, 0), 0)
    group = iota((rows, seqs), 1)
    in_owner = (position >= group * rows) & (position < (group + 1) * rows)
    in_home = (my_req >= group * rows) & (my_req < (group + 1) * rows)
    owner_hot = onehot(in_owner)
    home_hot = onehot(in_home)
    col_ids = iota((rows, rows), 1)
    rank_home = total_of(
        jnp.where(col_ids < row_ids, dot_t(owner_hot, owner_hot), 0.0), 1
    ).astype(jnp.int32)
    rank_slot = total_of(
        jnp.where(req_row < my_req, dot_t(home_hot, home_hot), 0.0), 1
    ).astype(jnp.int32)
    home_cell = total_of(jnp.where(in_owner, group, 0), 1) * BLOCK + rank_home
    slot_cell = total_of(jnp.where(in_home, group, 0), 1) * BLOCK + rank_slot
    lanes = iota((rows, cells), 1)
    home_lo, home_hi = lanes == home_cell, lanes == home_cell + CAP
    slot_lo, slot_hi = lanes == slot_cell, lanes == slot_cell + CAP

    tok = tokens_ref[...]
    pack[...] = (dot(turned(home_lo), tok[:, :half]) + dot(turned(home_hi), tok[:, half:])).astype(
        BF16
    )
    place = iota((BLOCK, rows), 0)
    source_row = iota((BLOCK, rows), 1)
    long_pack[...] = (
        dot(onehot((source_row == place) & (place < LONGS)), tok[:, :half])
        + dot(onehot((source_row + LONGS == place) & (place >= LONGS)), tok[:, half:])
    ).astype(BF16)

    pl.semaphore_wait(barrier, total - 1)

    def at_band(ref, index):
        return ref.at[pl.ds(pl.multiple_of(index * rows, rows), rows)]

    def band_copy(src, dst, source, target, send_sems, recv_sems):
        return pltpu.make_async_remote_copy(
            src_ref=src,
            dst_ref=at_band(dst, source),
            send_sem=send_sems.at[target],
            recv_sem=recv_sems.at[source],
            device_id=(seq, target),
            device_id_type=MESH,
        )

    def full_copy(target, source):
        return band_copy(tokens_ref, full, source, target, gssem, grsem)

    def sums_copy(target, source):
        return band_copy(at_band(sums, target), sums_recv, source, target, mssem, mrsem)

    peers = [lax.rem(head + k, heads) for k in range(1, heads)]
    sources = [lax.rem(head + heads - k, heads) for k in range(1, heads)]
    for peer in peers:
        full_copy(peer, head).start()
    own_full = pltpu.make_async_copy(tokens_ref, at_band(full, head), self_sem.at[4])
    own_full.start()

    def rows_copy(target, source):
        return pltpu.make_async_remote_copy(
            src_ref=at_block(pack, lax.rem(target, seqs)),
            dst_ref=at_block(recv, source),
            send_sem=ssem.at[target],
            recv_sem=rsem.at[source],
            device_id=device_of(target),
            device_id_type=MESH,
        )

    def long_copy(target, source_head):
        return pltpu.make_async_remote_copy(
            src_ref=long_pack,
            dst_ref=at_block(long_recv, source_head),
            send_sem=lssem.at[target],
            recv_sem=lrsem.at[source_head],
            device_id=device_of(target),
            device_id_type=MESH,
        )

    def send_long(k, carry):
        long_copy(lax.rem(me + k, total), head).start()
        return carry

    @pl.when(seq == 0)
    def _():
        lax.fori_loop(1, total, send_long, 0)
        own_long = pltpu.make_async_copy(long_pack, at_block(long_recv, head), self_sem.at[0])
        own_long.start()
        own_long.wait()

    def send(k, carry):
        rows_copy(lax.rem(me + k, total), me).start()
        return carry

    lax.fori_loop(1, total, send, 0)
    own_rows = pltpu.make_async_copy(at_block(pack, seq), at_block(recv, me), self_sem.at[1])
    own_rows.start()

    request_lanes = iota((1, requests), 1)
    my_piece = total_of(jnp.where(iota((1, seqs), 1) == seq, pieces_ref[...], 0), 1)
    long_owner = jnp.zeros_like(my_piece)
    for k in range(1, LONGS):
        long_owner = long_owner + jnp.where(my_piece >= k * piece_count, 1, 0)
    piece_index = my_piece - long_owner * piece_count
    long_len = total_of(jnp.where(request_lanes == long_owner, lengths_ref[...], 0), 1)
    long_limit = long_len - piece_index * piece_len

    all_len = jnp.concatenate([my_len, jnp.broadcast_to(long_len, (PAD, 1))], axis=0)
    angles = all_len.astype(F32) * freq_ref[...]
    lane128 = iota(angles.shape, 1)
    cosine = jnp.where(lane128 < ROT, jnp.cos(angles), 1.0)
    sine = jnp.sin(angles)
    sine_a = jnp.where(lane128 < ROT // 2, -sine, 0.0)
    sine_b = jnp.where((lane128 >= ROT // 2) & (lane128 < ROT), sine, 0.0)

    def spread_table(table, rest):
        filler = jnp.full((table.shape[0], HD - 128), rest, F32)
        return jnp.concatenate([table, filler] * heads_here, axis=1)

    cosine = spread_table(cosine, 1.0)
    sine_a = spread_table(sine_a, 0.0)
    sine_b = spread_table(sine_b, 0.0)

    def rotary(values, n):
        return (
            values * cosine[:n]
            + pltpu.roll(values, width_here - ROT // 2, 1) * sine_a[:n]
            + pltpu.roll(values, ROT // 2, 1) * sine_b[:n]
        )

    own_full.wait()
    for source in sources:
        full_copy(head, source).wait_recv()
    at_home = jnp.concatenate([full[h * rows : (h + 1) * rows, :] for h in range(heads)], axis=1)
    x2[...] = layer_norm(at_home.astype(F32), ln2_gain[...], ln2_shift[...]).astype(BF16)
    load_up.wait()
    matmul_into(up, x2, w_up, TILE)
    before = up[...] + b_up[...]
    hidden[...] = (0.5 * before * (1.0 + lax.erf(before * (0.5**0.5)))).astype(BF16)
    load_down.wait()
    matmul_into(down, hidden, w_down, TILE)
    for h in range(heads):
        sums[h * rows : (h + 1) * rows, :] = down[
            :, h * width_here : (h + 1) * width_here
        ].astype(BF16)

    own_rows.wait()

    def arrive(k, carry):
        rows_copy(me, lax.rem(me + total - k, total)).wait_recv()
        return carry

    lax.fori_loop(1, total, arrive, 0)
    for source_head in range(heads):

        @pl.when(jnp.logical_or(seq != 0, head != source_head))
        def _():
            long_copy(me, source_head).wait_recv()

    pick_lo, pick_hi = onehot(slot_lo), onehot(slot_hi)
    row8, col8 = iota((PAD, BLOCK), 0), iota((PAD, BLOCK), 1)
    long_lo = onehot((row8 == 0) & (col8 == long_owner))
    long_hi = onehot((row8 == 0) & (col8 == long_owner + LONGS))
    columns = []
    long_columns = []
    for h in range(heads):
        block = recv[h * cells : (h + 1) * cells, :]
        lblock = long_recv[h * BLOCK : (h + 1) * BLOCK, :]
        columns += [dot(pick_lo, block), dot(pick_hi, block)]
        long_columns += [dot(long_lo, lblock), dot(long_hi, lblock)]
    resident = jnp.concatenate(
        [jnp.concatenate(columns, axis=1), jnp.concatenate(long_columns, axis=1)], axis=0
    )
    x1[...] = layer_norm(resident, ln1_gain[...], ln1_shift[...]).astype(BF16)

    for peer in peers:
        sums_copy(peer, head).start()
    own_sums = pltpu.make_async_copy(at_band(sums, head), at_band(sums_recv, head), self_sem.at[5])
    own_sums.start()

    scale = HD ** (-0.5)
    load_q.wait()
    matmul_into(qkv.at[0], x1, w_qkv.at[0], TILE)
    query = rotary(qkv[0] + b_qkv[0:1, :], rows + PAD)
    lane_here = iota((PAD, width_here), 1)
    head_row = iota((PAD, width_here), 0)
    own_lanes = (lane_here >= head_row * HD) & (lane_here < (head_row + 1) * HD)
    long_query = jnp.where(own_lanes, query[rows : rows + 1], 0.0).astype(BF16)
    query = query[:rows].astype(BF16)
    load_kl.wait()
    scores = dot_t(long_query, kl[...]) * scale
    usable = iota(scores.shape, 1) < long_limit
    masked = jnp.where(usable, scores, very_low)
    piece_top = jnp.max(masked, axis=1, keepdims=True)
    weights = jnp.where(usable, jnp.exp(masked - piece_top), 0.0)
    piece_total = total_of(weights, 1)
    load_vl.wait()
    mixed = dot(weights.astype(BF16), vl[...])
    rowh = iota((PAD, HD), 0)
    piece_out = jnp.zeros((PAD, HD), F32)
    for h in range(heads_here):
        piece_out = jnp.where(rowh == h, mixed[:, h * HD : (h + 1) * HD], piece_out)
    stat_lane = iota((PAD, STATS), 1)
    part[...] = jnp.concatenate(
        [piece_out, jnp.where(stat_lane < STATS // 2, piece_top, piece_total)], axis=1
    )

    def part_copy(target, source):
        return pltpu.make_async_remote_copy(
            src_ref=part,
            dst_ref=at_block(part_recv, source),
            send_sem=pssem.at[target],
            recv_sem=prsem.at[source],
            device_id=(target, head),
            device_id_type=MESH,
        )

    def send_part(k, carry):
        part_copy(lax.rem(seq + k, seqs), seq).start()
        return carry

    lax.fori_loop(1, seqs, send_part, 0)
    own_part = pltpu.make_async_copy(part, at_block(part_recv, seq), self_sem.at[2])
    own_part.start()

    load_k.wait()
    matmul_into(qkv.at[1], x1, w_qkv.at[1], TILE)
    load_v.wait()
    matmul_into(qkv.at[2], x1, w_qkv.at[2], TILE)
    new_key = rotary(qkv[1][:rows] + b_qkv[1:2, :], rows).astype(BF16)
    new_value = (qkv[2][:rows] + b_qkv[2:3, :]).astype(BF16).astype(F32)
    product = query.astype(F32) * new_key.astype(F32)

    lane_q = iota((rows, width_here), 1)
    query32 = query.astype(F32)
    split = jnp.concatenate(
        [
            jnp.where((lane_q >= h * HD) & (lane_q < (h + 1) * HD), query32, 0.0)
            for h in range(heads_here)
        ],
        axis=0,
    ).astype(BF16)
    load_ks.wait()
    scores = dot_t(split, ks[...]) * scale
    first = jnp.concatenate([row_ids * short_max] * heads_here, axis=0)
    count = jnp.where(my_len <= short_max, my_len, 0)
    last = first + jnp.concatenate([count] * heads_here, axis=0)
    column = iota(scores.shape, 1)
    usable = (column >= first) & (column < last)
    masked = jnp.where(usable, scores, very_low)
    short_top = jnp.max(masked, axis=1, keepdims=True)
    weights = jnp.where(usable, jnp.exp(masked - short_top), 0.0)
    short_total = total_of(weights, 1)
    load_vs.wait()
    short_out = dot(weights.astype(BF16), vs[...])

    own_part.wait()

    def part_arrive(k, carry):
        part_copy(seq, lax.rem(seq + seqs - k, seqs)).wait_recv()
        return carry

    lax.fori_loop(1, seqs, part_arrive, 0)
    expand = onehot(
        (iota((seqs, cells), 1) >= BLOCK * iota((seqs, cells), 0))
        & (iota((seqs, cells), 1) < BLOCK * iota((seqs, cells), 0) + BLOCK)
    )
    piece_lane = dot(
        jnp.broadcast_to(pieces_ref[...].astype(F32), (PAD, seqs)).astype(BF16), expand
    )[0:1, :]
    first_lane = my_req.astype(F32) * piece_count
    matches = (piece_lane >= first_lane) & (piece_lane < first_lane + piece_count)
    stats = part_recv[:, HD:].T
    tops, totals = stats[0:1, :], stats[STATS // 2 : STATS // 2 + 1, :]
    place_in = lax.bitwise_and(lanes, BLOCK - 1)
    for h in range(heads_here):
        here = slice(h * HD, (h + 1) * HD)
        band = slice(h * rows, (h + 1) * rows)
        own_score = total_of(product[:, here], 1) * scale
        pick = matches & (place_in == h)
        spread = jnp.where(pick, tops, very_low)
        summit = jnp.maximum(
            jnp.maximum(short_top[band], own_score), jnp.max(spread, axis=1, keepdims=True)
        )
        piece_scale = jnp.where(pick, jnp.exp(spread - summit), 0.0)
        short_scale = jnp.exp(short_top[band] - summit)
        own_scale = jnp.exp(own_score - summit)
        denominator = (
            short_total[band] * short_scale + own_scale + total_of(piece_scale * totals, 1)
        )
        numerator = (
            short_out[band, here] * short_scale
            + new_value[:, here] * own_scale
            + dot(piece_scale, part_recv[:, :HD], precision=lax.Precision.HIGHEST)
        )
        attended[:, here] = (numerator / denominator).astype(BF16)
    load_d.wait()
    matmul_into(dense, attended, w_dense, TILE)

    give_lo, give_hi = turned(slot_lo), turned(slot_hi)
    for h in range(heads):
        cols = slice(h * width_here, h * width_here + half)
        rest = slice(h * width_here + half, (h + 1) * width_here)
        back[h * cells : (h + 1) * cells, :] = (
            dot(give_lo, dense[:, cols].astype(BF16))
            + dot(give_hi, dense[:, rest].astype(BF16))
        ).astype(BF16)

    def back_copy(target, source):
        return pltpu.make_async_remote_copy(
            src_ref=at_block(back, target),
            dst_ref=at_block(back_recv, source),
            send_sem=bssem.at[target],
            recv_sem=brsem.at[source],
            device_id=device_of(target),
            device_id_type=MESH,
        )

    def send_back(k, carry):
        back_copy(lax.rem(me + k, total), me).start()
        return carry

    lax.fori_loop(1, total, send_back, 0)
    own_back = pltpu.make_async_copy(at_block(back, me), at_block(back_recv, me), self_sem.at[3])
    own_back.start()

    def sent(k, carry):
        target = lax.rem(me + k, total)
        rows_copy(target, me).wait_send()
        return carry

    lax.fori_loop(1, total, sent, 0)

    def sent_part(k, carry):
        part_copy(lax.rem(seq + k, seqs), seq).wait_send()
        return carry

    lax.fori_loop(1, seqs, sent_part, 0)

    def sent_long(k, carry):
        long_copy(lax.rem(me + k, total), head).wait_send()
        return carry

    @pl.when(seq == 0)
    def _():
        lax.fori_loop(1, total, sent_long, 0)

    own_back.wait()
    own_sums.wait()
    for peer in peers:
        full_copy(peer, head).wait_send()
        sums_copy(peer, head).wait_send()
    settled = tokens_ref[...].astype(F32) + b_dense[...] + b_down[...]
    for source in sources:
        sums_copy(head, source).wait_recv()
    for h in range(heads):
        settled = settled + sums_recv[h * rows : (h + 1) * rows, :].astype(F32)

    def back_arrive(k, carry):
        back_copy(lax.rem(me + k, total), me).wait_send()
        back_copy(me, lax.rem(me + total - k, total)).wait_recv()
        return carry

    lax.fori_loop(1, total, back_arrive, 0)
    take_lo, take_hi = onehot(home_lo), onehot(home_hi)
    low = jnp.zeros((rows, half), F32)
    high = jnp.zeros((rows, half), F32)
    for h in range(heads):
        block = back_recv[h * cells : (h + 1) * cells, :]
        low = low + dot(take_lo, block)
        high = high + dot(take_hi, block)
    out_ref[...] = (settled + jnp.concatenate([low, high], axis=1)).astype(BF16)


TILE = 1024


def local(
    seqs,
    heads,
    tokens,
    ln1_gain,
    ln1_shift,
    ln2_gain,
    ln2_shift,
    w_qkv,
    b_qkv,
    w_dense,
    b_dense,
    w_up,
    b_up,
    w_down,
    b_down,
    keys_short,
    values_short,
    keys_long,
    values_long,
    lengths,
    slot_request,
    piece_map,
):
    total = seqs * heads
    rows, width_here = tokens.shape
    width = width_here * heads
    units = w_up.shape[1]
    half = width_here // 2
    short_rows = rows * keys_short.shape[1]
    exponent = -2.0 * (np.arange(128) % (ROT // 2)) / ROT
    freq = jnp.asarray(np.power(10000.0, exponent).astype(np.float32)[None])
    vmem = pl.BlockSpec(memory_space=pltpu.VMEM)
    hbm = pl.BlockSpec(memory_space=pl.ANY)
    dma = pltpu.SemaphoreType.DMA
    return pl.pallas_call(
        functools.partial(layer_kernel, seqs, heads),
        out_shape=jax.ShapeDtypeStruct((rows, width_here), BF16),
        in_specs=[vmem] * 13 + [hbm] * 8,
        out_specs=vmem,
        scratch_shapes=[
            pltpu.VMEM((3, width, width_here), BF16),
            pltpu.VMEM((width_here, width), BF16),
            pltpu.VMEM((width, units), BF16),
            pltpu.VMEM((units, width), BF16),
            pltpu.VMEM((short_rows, width_here), BF16),
            pltpu.VMEM((short_rows, width_here), BF16),
            pltpu.VMEM(keys_long.shape, BF16),
            pltpu.VMEM(values_long.shape, BF16),
            pltpu.VMEM((seqs * BLOCK, half), BF16),
            pltpu.VMEM((total * BLOCK, half), BF16),
            pltpu.VMEM((BLOCK, half), BF16),
            pltpu.VMEM((heads * BLOCK, half), BF16),
            pltpu.VMEM((PAD, HD + STATS), F32),
            pltpu.VMEM((seqs * PAD, HD + STATS), F32),
            pltpu.VMEM((total * BLOCK, half), BF16),
            pltpu.VMEM((total * BLOCK, half), BF16),
            pltpu.VMEM((rows + PAD, width), BF16),
            pltpu.VMEM((rows, width), BF16),
            pltpu.VMEM((3, rows + PAD, width_here), F32),
            pltpu.VMEM((rows, units), F32),
            pltpu.VMEM((rows, units), BF16),
            pltpu.VMEM((rows, width_here), BF16),
            pltpu.VMEM((rows, width), F32),
            pltpu.VMEM((rows, width), F32),
            pltpu.VMEM((heads * rows, width_here), BF16),
            pltpu.VMEM((heads * rows, width_here), BF16),
            pltpu.VMEM((heads * rows, width_here), BF16),
            dma((10,)),
            dma((6,)),
            dma((heads,)),
            dma((heads,)),
            dma((heads,)),
            dma((heads,)),
            dma((total,)),
            dma((total,)),
            dma((total,)),
            dma((heads,)),
            dma((seqs,)),
            dma((seqs,)),
            dma((total,)),
            dma((total,)),
        ],
        compiler_params=pltpu.CompilerParams(
            collective_id=0, has_side_effects=True, vmem_limit_bytes=66_500_000
        ),
        name="layer",
    )(
        tokens,
        slot_request[None],
        lengths[None],
        piece_map[None],
        freq,
        ln1_gain[None],
        ln1_shift[None],
        ln2_gain[None],
        ln2_shift[None],
        b_qkv,
        b_dense[None],
        b_down[None],
        b_up[None],
        jnp.transpose(w_qkv, (1, 0, 2)),
        w_dense,
        w_up,
        w_down,
        keys_short.reshape(short_rows, width_here),
        values_short.reshape(short_rows, width_here),
        keys_long,
        values_long,
    )


def solution(mesh):
    in_specs = (
        P("seq", "head"),
        P(),
        P(),
        P(),
        P(),
        P(None, None, "head"),
        P(None, "head"),
        P("head", None),
        P("head"),
        P(None, "head"),
        P("head"),
        P("head", None),
        P("head"),
        P("seq", None, "head"),
        P("seq", None, "head"),
        P("seq", "head"),
        P("seq", "head"),
        P(),
        P(),
        P(),
    )
    out_specs = P("seq", "head")
    body = functools.partial(local, mesh.shape["seq"], mesh.shape["head"])
    return jax.shard_map(body, mesh=mesh, in_specs=in_specs, out_specs=out_specs, check_vma=False)
```
